128 devices in a mesh: lat: 4 (over z_hi, core), lon: 32 (over y, x, z_lo).
Axes of the slice: x: 4, y: 4, z: 4 (z_hi: 2, z_lo: 2; z = z_hi * 2 + z_lo), core: 2. Of those that a mesh axis runs over, the one named last changes fastest.
Arguments:
- obs_feat: bfloat16 [131072, 256], P(('lat', 'lon')), may hold values from -6 to 6
- obs_owner: int32 [131072, 1], P(('lat', 'lon')), may hold values from 0 to 127; in each aligned block of 1024 rows (0 to 1023, 1024 to 2047, ...) at most 16 rows name the same one
- obs_cell: int32 [131072], P(('lat', 'lon')), may hold values from 0 to 1023
- obs_valid: int32 [131072], P(('lat', 'lon')), may hold values 0 or 1
- grid_feat: bfloat16 [64, 2048, 512], P('lat', 'lon'), may hold values from -6 to 6
- w_embed: bfloat16 [256, 512], replicated, may hold values from -0.375 to 0.375
- gains: float32 [2, 512], replicated, may hold values from 0.5 to 1.5
- w_query: bfloat16 [2, 512, 512], replicated, may hold values from -2.4748737 to 2.4748737
- w_key: bfloat16 [2, 512, 512], replicated, may hold values from -2.4748737 to 2.4748737
- w_value: bfloat16 [2, 512, 512], replicated, may hold values from -0.25 to 0.25
- w_out: bfloat16 [2, 512, 512], replicated, may hold values from -0.25 to 0.25
Outputs:
- encoded: bfloat16 [64, 2048, 512], P('lat', 'lon')
The draws below stay inside these ranges and needn't reach their ends.
Inputs may be any that keep to these rules, and one draw needn't show every extreme that they name: `obs_owner`: owner d is the device of latitude index d // 32 and longitude index d % 32. Among the rows of one device no owner appears more than 16 times, and in some device one owner appears exactly 16 times. `obs_cell`: cell r * 64 + c is row r and column c of the owner's tile.
All inputs are finite; a program needn't handle non-finite values. No bound on the sum of `obs_valid` on one device may be relied on, other than what follows from the above.
Results may differ from the reference program's by a relative error of at most 0.015.
The reference program's roundings to bfloat16 on the way (of `embedded`, `normed`, `weights` and `attended`) count: a program that leaves them out, or rounds other values in their place, can miss the bound.
Values may be sent and summed in bfloat16 or wider, within the bound.
No kernel may reach another device: no remote copies, remote signals or barrier semaphores. Data moves between devices by JAX's collectives and lax.ppermute only.
A program may use at most 192 MiB of HBM per device.

```python
import math
import jax
import jax.numpy as jnp
import numpy as np
from jax import lax

D = 512
HEADS = 8
FIN = 256
LAYERS = 2
CLAT = 16
CLON = 64
OBS_DEV = 1024
CAP = 16
NLAT = 64
NLON = 2048
OBS_ALL = 131072
N_LON = 32
DEVICES = 128


def drawn_weight(own_key):
    base = jnp.clip(jax.random.normal(own_key, (LAYERS, D, D), jnp.float32), -4.0, 4.0)
    return base * (2.0 * D ** (-0.5))


def draw_w_query(key, part):
    base = drawn_weight(jax.random.fold_in(key, 11))
    return base.astype(jnp.bfloat16)


def draw_w_key(key, part):
    base = drawn_weight(jax.random.fold_in(key, 23))
    return base.astype(jnp.bfloat16)


def touch_ends(values, key, smallest, high):
    extent = values.shape
    place = [jax.random.randint(jax.random.fold_in(key, axis), (), 0, extent[axis]) for axis in range(len(extent))]
    values = values.at[tuple(place)].set(smallest)
    longest = extent.index(max(extent))
    place[longest] = (place[longest] + 1) % extent[longest]
    return values.at[tuple(place)].set(high)


def level_of(stream_key, shape, cuts, least, largest):
    gain = 1.0
    for dim, blocks in cuts:
        heights = jax.random.uniform(jax.random.fold_in(jax.random.fold_in(stream_key, 6), dim), (blocks,), jnp.float32, least / len(cuts), largest / len(cuts))
        gain = gain * jnp.repeat(jnp.exp(heights), shape[dim] // blocks).reshape((-1,) + (1,) * (len(shape) - 1 - dim))
    return gain


def assign_block(key, own, number, rows, amount, top, reach, slope):
    order = jax.random.permutation(key, amount)
    crowded, common = load_shares(amount, rows * top, reach, slope, True), load_shares(amount, rows * top, reach, slope, False)
    places = jnp.arange(amount)

    def named(sizes, rotation):
        used = int((sizes > 0).sum())
        fixed = max(1, used // 4)
        shifted = fixed + (places - fixed + rotation * (used - fixed)) % max(1, amount - fixed)
        return jnp.zeros((amount,), jnp.int32).at[order[jnp.where(places < fixed, places, shifted)]].set(jnp.asarray(sizes, jnp.int32))

    sizes = jnp.where(number % 4 == 0, named(crowded, number // 4), named(common, number - number // 4 - 1))
    mixed = jax.random.permutation(jax.random.fold_in(own, 3), amount)
    giver, taker = mixed[0:amount // 2 * 2:2], mixed[1:amount // 2 * 2:2]
    room = jnp.minimum(sizes[giver] - 1, reach - sizes[taker]) // 2
    room = jnp.where((giver == order[0]) | (taker == order[0]) | (sizes[taker] == 0), 0, jnp.maximum(room, 0))
    shifted = jax.random.randint(jax.random.fold_in(own, 4), (amount // 2,), 0, 1 << 20) % (room + 1)
    sizes = sizes.at[giver].add(-shifted).at[taker].add(shifted)
    labels = jnp.searchsorted(jnp.cumsum(sizes), jnp.arange(rows * top), side="right").astype(jnp.int32)
    table = labels.reshape(top, rows).T
    table = table[jax.random.permutation(jax.random.fold_in(own, 1), rows)]
    rotation = jax.random.randint(jax.random.fold_in(own, 2), (rows, 1), 0, top)
    return jnp.take_along_axis(table, (jnp.arange(top)[None, :] + rotation) % top, axis=1)


def load_shares(count, total, limit, skew, full):
    portions = [(1 << 20) // math.isqrt(standing ** skew) + 1 for standing in range(1, count + 1)]
    largest = limit if full else min(limit, max(-(-total // count), total * portions[0] // sum(portions)))
    least = 1 if total - largest >= count - 1 else 0
    holding, rest = [largest] + [least] * (count - 1), total - largest - least * (count - 1)
    while rest > 0:
        free = [i for i in range(1, count) if holding[i] < largest] or [i for i in range(1, count) if holding[i] < limit]
        whole, left = sum([portions[i] for i in free]), rest
        for i in free:
            extra = min(limit - holding[i], max(1, left * portions[i] // whole), rest)
            holding[i] = holding[i] + extra
            rest = rest - extra
    return np.array(holding)


def gaussian(stream_key, extent, spread, most, split=(), kind=jnp.bfloat16):
    level = level_of(stream_key, extent, split, -0.22, 0.18) if split else 1.0
    values = jax.random.normal(stream_key, extent, jnp.float32) * spread * level
    return jnp.minimum(jnp.maximum(values, -most), most).astype(kind)


def setup_inputs(seed: int = 0) -> dict:
    arg_keys = jax.random.split(jax.random.key(seed), 12)
    obs_feat = gaussian(arg_keys[0], (OBS_ALL, FIN), 1.0, 6.0, ((0, 128),))
    obs_owner_keys = jax.random.split(jax.random.fold_in(arg_keys[1], 1), OBS_ALL // OBS_DEV)
    obs_owner_turns = jax.random.permutation(jax.random.fold_in(arg_keys[1], 3), OBS_ALL // OBS_DEV)
    obs_owner = jax.vmap(lambda own, number: assign_block(jax.random.fold_in(arg_keys[1], 2), own, number, OBS_DEV, DEVICES, 1, CAP, 2))(obs_owner_keys, obs_owner_turns).reshape((OBS_ALL, 1))
    obs_cell = touch_ends(jax.random.randint(arg_keys[2], (OBS_ALL,), 0, CLAT * CLON), jax.random.fold_in(arg_keys[2], 1), 0, (CLAT * CLON) - 1).astype(jnp.int32)
    obs_valid = touch_ends((jax.random.randint(arg_keys[3], (OBS_ALL,), 0, 4) < 3).astype(jnp.int32), jax.random.fold_in(arg_keys[3], 1), 0, 1)
    grid_feat = gaussian(arg_keys[4], (NLAT, NLON, D), 1.0, 6.0, ((0, 4), (1, 32)))
    w_embed = gaussian(arg_keys[5], (FIN, D), FIN ** -0.5, 0.375)
    gains = jnp.clip(1.0 + 0.1 * jax.random.normal(arg_keys[6], (LAYERS, D), jnp.float32), 0.5, 1.5)
    w_query = draw_w_query(jax.random.fold_in(arg_keys[11], 71), 0)
    w_key = draw_w_key(jax.random.fold_in(arg_keys[11], 71), 0)
    w_value = gaussian(arg_keys[9], (LAYERS, D, D), D ** -0.5, 0.25)
    w_out = gaussian(arg_keys[10], (LAYERS, D, D), D ** -0.5, 0.25)
    return dict(obs_feat=obs_feat, obs_owner=obs_owner, obs_cell=obs_cell, obs_valid=obs_valid, grid_feat=grid_feat, w_embed=w_embed, gains=gains, w_query=w_query, w_key=w_key, w_value=w_value, w_out=w_out)


def attend(query, keys, values, lat_first):
    width = query.shape[1]
    model_width = query.shape[2]
    head_size = model_width // HEADS
    blocks_row = width // 8
    q_five = query.astype(jnp.float32).reshape(8, blocks_row, 8, HEADS, head_size)

    def tiles_of(array):
        tiles = array.reshape(24, blocks_row + 2, 8, model_width)
        stacked = jnp.stack([tiles[:, j:j + blocks_row] for j in range(3)], axis=2)
        return stacked.reshape(24, blocks_row, 24, HEADS, head_size).astype(jnp.float32)
    key_tiles = tiles_of(keys)
    value_tiles = tiles_of(values)
    scores = jnp.einsum('anbhe,cnkhe->nhabck', q_five, key_tiles) * head_size ** (-0.5)
    rows_global = lat_first + jnp.arange(24, dtype=jnp.int32)
    inside = (rows_global >= 0) & (rows_global < NLAT)
    scores = jnp.where(inside[:, None], scores, jnp.float32(-1e+30))
    flat = scores.reshape(blocks_row, HEADS, 64, 576)
    highest = lax.optimization_barrier(jnp.max(flat, axis=-1, keepdims=True))
    expo = jnp.exp(flat - highest)
    weights = (expo / lax.optimization_barrier(jnp.sum(expo, axis=-1, keepdims=True))).astype(jnp.bfloat16)
    weights = weights.reshape(blocks_row, HEADS, 8, 8, 24, 24).astype(jnp.float32)
    result = jnp.einsum('nhabck,cnkhe->anbhe', weights, value_tiles)
    return result.astype(jnp.bfloat16).reshape(8, width, model_width)

def reference(obs_feat, obs_owner, obs_cell, obs_valid, grid_feat, w_embed, gains, w_query, w_key, w_value, w_out):
    model_width = grid_feat.shape[2]

    def embed_block(block):
        return jax.nn.gelu(jnp.dot(block, w_embed, preferred_element_type=jnp.float32)).astype(jnp.bfloat16)
    embedded = lax.map(embed_block, obs_feat.reshape(DEVICES, OBS_DEV, FIN)).reshape(OBS_ALL, model_width)
    owner = obs_owner[:, 0]
    grid_row = owner // N_LON * CLAT + obs_cell // CLON
    grid_col = owner % N_LON * CLON + obs_cell % CLON
    total_cells = NLAT * NLON
    index = jnp.where(obs_valid == 1, grid_row * NLON + grid_col, total_cells).astype(jnp.int32)
    sums = jax.ops.segment_sum(embedded.astype(jnp.float32), index, num_segments=total_cells + 1)[:total_cells]
    counts = jax.ops.segment_sum(jnp.ones(index.shape, jnp.float32), index, num_segments=total_cells + 1)[:total_cells]
    hidden = (sums / jnp.maximum(counts, 1.0)[:, None]).reshape(NLAT, NLON, model_width) + grid_feat.astype(jnp.float32)
    for layer in range(LAYERS):
        scale = lax.rsqrt(lax.optimization_barrier(jnp.mean(hidden * hidden, axis=-1, keepdims=True)) + 1e-06)
        normed = (hidden * scale * gains[layer]).astype(jnp.bfloat16)
        flat = normed.reshape(-1, model_width)
        query = jnp.dot(flat, w_query[layer], preferred_element_type=jnp.float32).astype(jnp.bfloat16).reshape(NLAT, NLON, model_width)
        keys = jnp.dot(flat, w_key[layer], preferred_element_type=jnp.float32).astype(jnp.bfloat16).reshape(NLAT, NLON, model_width)
        values = jnp.dot(flat, w_value[layer], preferred_element_type=jnp.float32).astype(jnp.bfloat16).reshape(NLAT, NLON, model_width)

        def frame(array):
            wrapped = jnp.concatenate([array[:, -8:], array, array[:, :8]], axis=1)
            return jnp.pad(wrapped, ((8, 8), (0, 0), (0, 0)))
        key_pad = frame(keys)
        value_pad = frame(values)

        def one_row(index_row):
            start = index_row * 8
            query_rows = lax.dynamic_slice_in_dim(query, start, 8, 0)
            key_rows = lax.dynamic_slice_in_dim(key_pad, start, 24, 0)
            value_rows = lax.dynamic_slice_in_dim(value_pad, start, 24, 0)
            return attend(query_rows, key_rows, value_rows, start - 8)
        attended = lax.map(one_row, jnp.arange(NLAT // 8, dtype=jnp.int32)).reshape(NLAT, NLON, model_width)
        update = jnp.dot(attended.reshape(-1, model_width), w_out[layer], preferred_element_type=jnp.float32)
        hidden = hidden + update.reshape(NLAT, NLON, model_width)
    return hidden.astype(jnp.bfloat16)
```

```python
import jax
import jax.numpy as jnp
from jax import lax
from jax.experimental import pallas as pl
from jax.experimental.pallas import tpu as pltpu
from jax.sharding import PartitionSpec as P

HEADS = 8
LAYERS = 2
D = 512
FIN = 256
DEVICES = 128
CAP = 16
ROWS = 40
OBS = 1024
CELLS = 1024
SLOTS = DEVICES * CAP
BLOCK = 64
BANDS = 2
SECTORS = 8
FRAME = SECTORS + 2
GROUP = 256
KEYS = 9 * BLOCK
NEG = -1e30
F32 = jnp.float32
BF16 = jnp.bfloat16

VMEM = pl.BlockSpec(memory_space=pltpu.VMEM)
SMEM = pl.BlockSpec(memory_space=pltpu.SMEM)
ANY = pl.BlockSpec(memory_space=pl.ANY)
PARAMS = pltpu.CompilerParams(vmem_limit_bytes=56 * 1024 * 1024)
NT = (((1,), (1,)), ((), ()))


def iota(shape, axis):
    return lax.broadcasted_iota(jnp.int32, shape, axis)


def dispatch_kernel(owner_ref, cell_ref, valid_ref, feat_ref, send_ref):
    owner = owner_ref[...]
    cell = cell_ref[...]
    valid = valid_ref[...]
    wide = 256
    earlier = (iota((wide, wide), 0) < iota((wide, wide), 1)).astype(F32).astype(BF16)
    carry = jnp.zeros((DEVICES, 1), F32)
    ranks = []
    chosen = []
    for at in range(0, OBS, wide):
        hot = (iota((DEVICES, wide), 0) == owner[:, at : at + wide]).astype(F32)
        before = jnp.dot(hot.astype(BF16), earlier, preferred_element_type=F32) + carry
        ranks.append(jnp.sum(hot * before, axis=0, keepdims=True))
        carry = carry + jnp.sum(hot, axis=1, keepdims=True)
        chosen.append(hot.astype(BF16))
    rank = jnp.concatenate(ranks, axis=1).astype(jnp.int32)
    hot_all = jnp.concatenate(chosen, axis=1)
    row = cell // 64
    col = cell % 64
    high = (row // 8) * SECTORS + col // 8 + 1
    low = (row % 8) * 8 + col % 8
    usable = valid == 1
    high = jnp.where(usable, high, 0)
    low = jnp.where(usable, low, 0)
    lane = iota((128, OBS), 0)
    part = jnp.where(lane < CAP, high, jnp.where(lane < 2 * CAP, low, 0))
    entry = jnp.where(lane % CAP == rank, part, 0).astype(F32).astype(BF16)
    tags = lax.dot_general(hot_all, entry, NT, preferred_element_type=F32)
    send_ref[:, 32:40, :] = jnp.broadcast_to(tags[:, None, :], (DEVICES, 8, 128)).astype(BF16)
    target = owner * CAP + rank
    feat = feat_ref[...]
    step = 256
    for at in range(0, SLOTS, step):
        pick = (iota((step, OBS), 0) + at == target).astype(F32).astype(BF16)
        rows = jnp.dot(pick, feat, preferred_element_type=F32).astype(BF16)
        first = at // CAP
        count = step // CAP
        send_ref[first : first + count, 0:16, :] = rows[:, :128].reshape(count, CAP, 128)
        send_ref[first : first + count, 16:32, :] = rows[:, 128:].reshape(count, CAP, 128)


def dispatch(owner, cell, valid, feat):
    return pl.pallas_call(
        dispatch_kernel,
        out_shape=jax.ShapeDtypeStruct((DEVICES, ROWS, 128), BF16),
        in_specs=[VMEM] * 4,
        out_specs=VMEM,
        compiler_params=PARAMS,
        name="dispatch",
    )(owner, cell, valid, feat)


def norm_rows(hidden, gain):
    scale = lax.rsqrt(jnp.mean(hidden * hidden, axis=-1, keepdims=True) + 1e-06)
    return (hidden * scale * gain).astype(BF16)


def combine_kernel(got_ref, embed_ref, grid_ref, gain_ref, hidden_ref, normed_ref, emb_ref, tag_ref):
    step = 512
    for at in range(0, SLOTS, step):
        first = at // CAP
        count = step // CAP
        left = got_ref[first : first + count, 0:16, :].reshape(step, 128)
        right = got_ref[first : first + count, 16:32, :].reshape(step, 128)
        raw = jnp.concatenate([left, right], axis=1)
        product = jnp.dot(raw, embed_ref[...], preferred_element_type=F32)
        emb_ref[at : at + step, :] = jax.nn.gelu(product).astype(BF16)
    tag_ref[...] = got_ref[:, 32:40, :].astype(F32).reshape(DEVICES * 8, 128)
    tags = tag_ref[pl.ds(0, DEVICES, stride=8), :]
    tags = jnp.transpose(tags)[: 2 * CAP].astype(BF16)
    spread = (iota((DEVICES, SLOTS), 1) // CAP == iota((DEVICES, SLOTS), 0)).astype(F32).astype(BF16)
    wide = jnp.dot(tags, spread, preferred_element_type=F32)
    own = iota((CAP, SLOTS), 1) % CAP == iota((CAP, SLOTS), 0)
    high = jnp.sum(jnp.where(own, wide[:CAP], 0.0), axis=0, keepdims=True)
    low = jnp.sum(jnp.where(own, wide[CAP:], 0.0), axis=0, keepdims=True)
    index = jnp.where(high > 0.5, (high - 1.0) * 64.0 + low, -1.0).astype(jnp.int32)
    size = 128
    for at in range(0, CELLS, size):
        hot = (iota((size, SLOTS), 0) + at == index).astype(F32)
        count = jnp.sum(hot, axis=1, keepdims=True)
        total = jnp.dot(hot.astype(BF16), emb_ref[...], preferred_element_type=F32)
        hidden_ref[at : at + size, :] = total / jnp.maximum(count, 1.0)
    for band in range(BANDS):
        for r in range(8):
            static = grid_ref[band * 8 + r].astype(F32)
            for sector in range(SECTORS):
                at = (band * SECTORS + sector) * BLOCK + r * 8
                hidden_ref[at : at + 8, :] += static[sector * 8 : sector * 8 + 8]
    gain = gain_ref[0:1, :]
    for at in range(0, CELLS, 128):
        normed_ref[at : at + 128, :] = norm_rows(hidden_ref[at : at + 128, :], gain)


def combine(got, w_embed, grid_feat, gains):
    return pl.pallas_call(
        combine_kernel,
        out_shape=(
            jax.ShapeDtypeStruct((CELLS, D), F32),
            jax.ShapeDtypeStruct((CELLS, D), BF16),
        ),
        in_specs=[VMEM] * 4,
        out_specs=(VMEM, VMEM),
        scratch_shapes=[pltpu.VMEM((SLOTS, D), BF16), pltpu.VMEM((DEVICES * 8, 128), F32)],
        compiler_params=PARAMS,
        name="combine",
    )(got, w_embed, grid_feat, gains)


def project_kernel(normed_ref, query_w, key_w, value_w, query_ref, key_ref, value_ref):
    flat = normed_ref[...]
    query = jnp.dot(flat, query_w[0], preferred_element_type=F32).astype(BF16)
    query_ref[...] = query * BF16(0.125)
    key_ref[...] = jnp.dot(flat, key_w[0], preferred_element_type=F32).astype(BF16)
    value_ref[...] = jnp.dot(flat, value_w[0], preferred_element_type=F32).astype(BF16)


def layer_spec(layer):
    return pl.BlockSpec((1, D, D), lambda i: (layer, 0, 0))


def project(normed, w_query, w_key, w_value, layer):
    whole = pl.BlockSpec((CELLS, D), lambda i: (0, 0))
    shape = jax.ShapeDtypeStruct((CELLS, D), BF16)
    return pl.pallas_call(
        project_kernel,
        grid=(1,),
        out_shape=(shape, shape, shape),
        in_specs=[whole] + [layer_spec(layer)] * 3,
        out_specs=(whole, whole, whole),
        compiler_params=PARAMS,
        name="project",
    )(normed, w_query, w_key, w_value)


def make_attend_kernel(last):
    def attend_kernel(
        lat_ref, query_ref, key_ref, value_ref, up_ref, down_ref, west_ref, east_ref,
        hidden_ref, gain_ref, key_w, value_w, out_w, *rest,
    ):
        if last:
            out_ref, key_f, value_f, att_ref, new_ref, sems = rest
        else:
            new_ref, normed_ref, key_f, value_f, att_ref, sems = rest
        copies = []
        for band in range(BANDS):
            for which, (source, frame) in enumerate(((key_ref, key_f), (value_ref, value_f))):
                copy = pltpu.make_async_copy(
                    source.at[pl.ds(band * SECTORS * BLOCK, SECTORS * BLOCK)],
                    frame.at[pl.ds(((band + 1) * FRAME + 1) * BLOCK, SECTORS * BLOCK)],
                    sems.at[band * 2 + which],
                )
                copy.start()
                copies.append(copy)
        for weight, frame in ((key_w, key_f), (value_w, value_f)):
            for source, row in ((up_ref, 0), (down_ref, BANDS + 1)):
                at = (row * FRAME + 1) * BLOCK
                frame[at : at + SECTORS * BLOCK, :] = jnp.dot(
                    source[...], weight[0], preferred_element_type=F32
                ).astype(BF16)
            for source, column in ((west_ref, 0), (east_ref, FRAME - 1)):
                done = jnp.dot(source[...], weight[0], preferred_element_type=F32).astype(BF16)
                for row in range(BANDS + 2):
                    at = (row * FRAME + column) * BLOCK
                    frame[at : at + BLOCK, :] = done[row * BLOCK : (row + 1) * BLOCK]
        for copy in copies:
            copy.wait()
        first = lat_ref[0] == 0
        final = lat_ref[0] == lat_ref[1] - 1
        lane_key = iota((1, KEYS), 1)

        def one_block(index, carry):
            band = index // SECTORS
            sector = index % SECTORS
            hide_top = jnp.where(first & (band == 0), 3 * BLOCK, 0)
            hide_low = jnp.where(final & (band == BANDS - 1), 6 * BLOCK, KEYS)
            bias = jnp.where((lane_key < hide_top) | (lane_key >= hide_low), NEG, 0.0).astype(F32)
            base = pl.multiple_of(index * BLOCK, BLOCK)
            corner = pl.multiple_of((band * FRAME + sector) * BLOCK, BLOCK)
            for group in range(2):
                lanes = slice(group * GROUP, (group + 1) * GROUP)
                query = query_ref[pl.ds(base, BLOCK), lanes]
                stacked = jnp.concatenate([query] * 4, axis=0)
                diagonal = iota((GROUP, GROUP), 0) // BLOCK == iota((GROUP, GROUP), 1) // BLOCK
                stacked = jnp.where(diagonal, stacked, jnp.zeros_like(stacked))
                keys = jnp.concatenate(
                    [key_f[pl.ds(corner + a * FRAME * BLOCK, 3 * BLOCK), lanes] for a in range(3)], axis=0
                )
                values = jnp.concatenate(
                    [value_f[pl.ds(corner + a * FRAME * BLOCK, 3 * BLOCK), lanes] for a in range(3)], axis=0
                )
                scores = lax.dot_general(stacked, keys, NT, preferred_element_type=F32) + bias
                highest = jnp.max(scores, axis=-1, keepdims=True)
                expo = jnp.exp(scores - highest)
                inverse = 1.0 / jnp.sum(expo, axis=-1, keepdims=True)
                weights = (expo * inverse).astype(BF16)
                mixed = jnp.dot(weights, values, preferred_element_type=F32)
                half = iota((BLOCK, 128), 1) < BLOCK
                for pair in range(2):
                    columns = slice(pair * 128, pair * 128 + 128)
                    low = mixed[pair * 128 : pair * 128 + BLOCK, columns]
                    high = mixed[pair * 128 + BLOCK : pair * 128 + 128, columns]
                    to = group * GROUP + pair * 128
                    att_ref[pl.ds(base, BLOCK), to : to + 128] = jnp.where(half, low, high).astype(BF16)
            return carry

        lax.fori_loop(0, BANDS * SECTORS, one_block, 0)
        gain = gain_ref[...]
        for at in range(0, CELLS, 256):
            update = jnp.dot(att_ref[at : at + 256, :], out_w[0], preferred_element_type=F32)
            hidden = hidden_ref[at : at + 256, :] + update
            new_ref[at : at + 256, :] = hidden
            if not last:
                normed_ref[at : at + 256, :] = norm_rows(hidden, gain)
        if last:
            for band in range(BANDS):
                for r in range(8):
                    pieces = []
                    for sector in range(SECTORS):
                        at = (band * SECTORS + sector) * BLOCK + r * 8
                        pieces.append(new_ref[at : at + 8, :])
                    out_ref[band * 8 + r] = jnp.concatenate(pieces, axis=0).astype(BF16)

    return attend_kernel


def attend(place, query, key, value, up, down, west, east, hidden, gain, w_key, w_value, w_out, layer):
    last = layer == LAYERS - 1

    def whole(shape):
        return pl.BlockSpec(shape, lambda i: (0,) * len(shape))

    cells = whole((CELLS, D))
    scratch = [
        pltpu.VMEM(((BANDS + 2) * FRAME * BLOCK, D), BF16),
        pltpu.VMEM(((BANDS + 2) * FRAME * BLOCK, D), BF16),
        pltpu.VMEM((CELLS, D), BF16),
    ]
    if last:
        scratch.append(pltpu.VMEM((CELLS, D), F32))
        out_shape = jax.ShapeDtypeStruct((16, 64, D), BF16)
        out_specs = whole((16, 64, D))
    else:
        out_shape = (jax.ShapeDtypeStruct((CELLS, D), F32), jax.ShapeDtypeStruct((CELLS, D), BF16))
        out_specs = (cells, cells)
    scratch.append(pltpu.SemaphoreType.DMA((4,)))
    halo = SECTORS * BLOCK
    side = (BANDS + 2) * BLOCK
    return pl.pallas_call(
        make_attend_kernel(last),
        grid=(1,),
        out_shape=out_shape,
        in_specs=[
            SMEM, cells, ANY, ANY,
            whole((halo, D)), whole((halo, D)), whole((side, D)), whole((side, D)),
            cells, whole((1, D)),
        ] + [layer_spec(layer)] * 3,
        out_specs=out_specs,
        scratch_shapes=scratch,
        compiler_params=PARAMS,
        name="attend",
    )(place, query, key, value, up, down, west, east, hidden, gain, w_key, w_value, w_out)


def neighbours(normed):
    lat_count = lax.axis_size("lat")
    lon_count = lax.axis_size("lon")
    halo = SECTORS * BLOCK
    rising = [(i, i + 1) for i in range(lat_count - 1)]
    falling = [(b, a) for a, b in rising]
    up = lax.ppermute(normed[halo:], "lat", rising)
    down = lax.ppermute(normed[:halo], "lat", falling)
    forward = [(i, (i + 1) % lon_count) for i in range(lon_count)]
    backward = [(b, a) for a, b in forward]
    edge = halo - BLOCK
    eastern = jnp.concatenate([up[edge:], normed[edge:halo], normed[halo + edge :], down[edge:]], axis=0)
    western = jnp.concatenate(
        [up[:BLOCK], normed[:BLOCK], normed[halo : halo + BLOCK], down[:BLOCK]], axis=0
    )
    west = lax.ppermute(eastern, "lon", forward)
    east = lax.ppermute(western, "lon", backward)
    return up, down, west, east


def local(
    obs_feat, obs_owner, obs_cell, obs_valid, grid_feat,
    w_embed, gains, w_query, w_key, w_value, w_out,
):
    send = dispatch(
        obs_owner.reshape(1, OBS), obs_cell.reshape(1, OBS), obs_valid.reshape(1, OBS), obs_feat
    )
    got = lax.all_to_all(send, ("lat", "lon"), split_axis=0, concat_axis=0, tiled=True)
    hidden, normed = combine(got, w_embed, grid_feat, gains)
    place = jnp.stack([lax.axis_index("lat"), jnp.int32(lax.axis_size("lat"))])
    for layer in range(LAYERS):
        up, down, west, east = neighbours(normed)
        query, key, value = project(normed, w_query, w_key, w_value, layer)
        following = min(layer + 1, LAYERS - 1)
        result = attend(
            place, query, key, value, up, down, west, east, hidden,
            gains[following : following + 1], w_key, w_value, w_out, layer,
        )
        if layer < LAYERS - 1:
            hidden, normed = result
    return result


def solution(mesh):
    placed = (
        P(("lat", "lon"), None),
        P(("lat", "lon"), None),
        P(("lat", "lon")),
        P(("lat", "lon")),
        P("lat", "lon", None),
        P(), P(), P(), P(), P(), P(),
    )
    return jax.shard_map(
        local, mesh=mesh, in_specs=placed, out_specs=P("lat", "lon", None), check_vma=False
    )
```

```python
import jax
import jax.numpy as jnp
from jax import lax
from jax.experimental import pallas as pl
from jax.experimental.pallas import tpu as pltpu
from jax.sharding import PartitionSpec as P

HEADS = 8
LAYERS = 2
D = 512
FIN = 256
DEVICES = 128
CAP = 16
ROWS = 40
OBS = 1024
CELLS = 1024
SLOTS = DEVICES * CAP
BLOCK = 64
BANDS = 2
SECTORS = 8
FRAME = SECTORS + 2
PAIRS = HEADS // 2
COLUMN = BANDS * BLOCK
EARLY = 5
NEG = -1e30
F32 = jnp.float32
BF16 = jnp.bfloat16

VMEM = pl.BlockSpec(memory_space=pltpu.VMEM)
SMEM = pl.BlockSpec(memory_space=pltpu.SMEM)
HBM = pl.BlockSpec(memory_space=pl.ANY)
PARAMS = pltpu.CompilerParams(vmem_limit_bytes=40 * 1024 * 1024)
WIDE = FRAME * BLOCK
HALO = SECTORS * BLOCK
NT = (((1,), (1,)), ((), ()))
TN = (((0,), (0,)), ((), ()))


def iota(shape, axis):
    return lax.broadcasted_iota(jnp.int32, shape, axis)


def dispatch_kernel(owner_ref, cell_ref, valid_ref, feat_hbm, send_ref, feat_ref, sem):
    fetch = pltpu.make_async_copy(feat_hbm, feat_ref, sem)
    fetch.start()
    owner = owner_ref[...]
    cell = cell_ref[...]
    valid = valid_ref[...]
    wide = 256
    earlier = (iota((wide, wide), 0) < iota((wide, wide), 1)).astype(F32).astype(BF16)
    carry = jnp.zeros((DEVICES, 1), F32)
    ranks = []
    chosen = []
    for at in range(0, OBS, wide):
        hot = (iota((DEVICES, wide), 0) == owner[:, at : at + wide]).astype(F32)
        before = jnp.dot(hot.astype(BF16), earlier, preferred_element_type=F32) + carry
        ranks.append(jnp.sum(hot * before, axis=0, keepdims=True))
        carry = carry + jnp.sum(hot, axis=1, keepdims=True)
        chosen.append(hot.astype(BF16))
    rank = jnp.concatenate(ranks, axis=1).astype(jnp.int32)
    hot_all = jnp.concatenate(chosen, axis=1)
    row = cell // 64
    col = cell % 64
    high = (col // 8) * BANDS + row // 8 + 1
    low = (row % 8) * 8 + col % 8
    usable = valid == 1
    high = jnp.where(usable, high, 0)
    low = jnp.where(usable, low, 0)
    lane = iota((128, OBS), 0)
    part = jnp.where(lane < CAP, high, jnp.where(lane < 2 * CAP, low, 0))
    entry = jnp.where(lane % CAP == rank, part, 0).astype(F32).astype(BF16)
    tags = lax.dot_general(hot_all, entry, NT, preferred_element_type=F32)
    send_ref[:, 32:40, :] = jnp.broadcast_to(tags[:, None, :], (DEVICES, 8, 128)).astype(BF16)
    target = owner * CAP + rank
    fetch.wait()
    feat = feat_ref[...]
    step = 256
    for at in range(0, SLOTS, step):
        pick = (iota((step, OBS), 0) + at == target).astype(F32).astype(BF16)
        rows = jnp.dot(pick, feat, preferred_element_type=F32).astype(BF16)
        first = at // CAP
        count = step // CAP
        send_ref[first : first + count, 0:16, :] = rows[:, :128].reshape(count, CAP, 128)
        send_ref[first : first + count, 16:32, :] = rows[:, 128:].reshape(count, CAP, 128)


def dispatch(owner, cell, valid, feat):
    return pl.pallas_call(
        dispatch_kernel,
        out_shape=jax.ShapeDtypeStruct((DEVICES, ROWS, 128), BF16),
        in_specs=[VMEM] * 3 + [HBM],
        out_specs=VMEM,
        scratch_shapes=[pltpu.VMEM((OBS, FIN), BF16), pltpu.SemaphoreType.DMA],
        compiler_params=PARAMS,
        name="dispatch",
    )(owner, cell, valid, feat)


def on_chip(array):
    return pltpu.with_memory_space_constraint(array, pltpu.VMEM)


def off_chip(array):
    return pltpu.with_memory_space_constraint(array, pltpu.HBM)


def norm_rows(hidden, gain):
    scale = lax.rsqrt(jnp.mean(hidden * hidden, axis=-1, keepdims=True) + 1e-06)
    return (hidden * scale * gain).astype(BF16)


def store_normed(at, rows, normed_ref, west_ref, east_ref):
    size = rows.shape[0]
    normed_ref[at : at + size, :] = rows
    for edge_ref, start in ((west_ref, 0), (east_ref, CELLS - COLUMN)):
        low = max(at, start)
        high = min(at + size, start + COLUMN)
        if low < high:
            edge_ref[low - start : high - start, :] = rows[low - at : high - at]


NORMED_SHAPES = (
    pltpu.VMEM((CELLS, D), BF16),
    pltpu.VMEM((BANDS * BLOCK, D), BF16),
    pltpu.VMEM((BANDS * BLOCK, D), BF16),
)


def combine_kernel(
    got_ref, embed_hbm, grid_hbm, gain_ref, hidden_ref, normed_ref, west_ref, east_ref,
    emb_ref, tag_ref, hot_ref, embed_ref, grid_ref, sems,
):
    fetch_embed = pltpu.make_async_copy(embed_hbm, embed_ref, sems.at[0])
    fetch_grid = pltpu.make_async_copy(grid_hbm, grid_ref, sems.at[1])
    fetch_embed.start()
    fetch_grid.start()
    tag_ref[...] = got_ref[:, 32:40, :].astype(F32).reshape(DEVICES * 8, 128)
    tags = tag_ref[pl.ds(0, DEVICES, stride=8), :]
    tags = jnp.transpose(tags)[: 2 * CAP].astype(BF16)
    spread = (iota((DEVICES, SLOTS), 1) // CAP == iota((DEVICES, SLOTS), 0)).astype(F32).astype(BF16)
    wide = jnp.dot(tags, spread, preferred_element_type=F32)
    own = iota((CAP, SLOTS), 1) % CAP == iota((CAP, SLOTS), 0)
    high = jnp.sum(jnp.where(own, wide[:CAP], 0.0), axis=0, keepdims=True)
    low = jnp.sum(jnp.where(own, wide[CAP:], 0.0), axis=0, keepdims=True)
    low_hot = (iota((BLOCK, SLOTS), 0).astype(F32) == low).astype(F32).astype(BF16)
    high_hot = (iota((16, SLOTS), 0).astype(F32) + 1.0 == high).astype(F32).astype(BF16)
    counts = lax.dot_general(low_hot, high_hot, NT, preferred_element_type=F32)
    inverse = 1.0 / jnp.maximum(counts, 1.0)
    high16 = jnp.broadcast_to(high, (16, SLOTS))
    for block in range(BANDS * SECTORS):
        mask = (high16 == block + 1.0).astype(F32).astype(BF16)
        for part in range(BLOCK // 16):
            at = block * BLOCK + part * 16
            hot_ref[at : at + 16, :] = low_hot[part * 16 : part * 16 + 16] * mask
    fetch_embed.wait()
    step = 512
    for at in range(0, SLOTS, step):
        first = at // CAP
        count = step // CAP
        left = got_ref[first : first + count, 0:16, :].reshape(step, 128)
        right = got_ref[first : first + count, 16:32, :].reshape(step, 128)
        raw = jnp.concatenate([left, right], axis=1)
        product = jnp.dot(raw, embed_ref[...], preferred_element_type=F32)
        emb_ref[at : at + step, :] = jax.nn.gelu(product).astype(BF16)
    gain = gain_ref[0:1, :]
    fetch_grid.wait()
    chunk = 512
    for start in range(0, CELLS, chunk):
        total = jnp.dot(hot_ref[start : start + chunk, :], emb_ref[...], preferred_element_type=F32)
        for sub in range(chunk // BLOCK):
            block = start // BLOCK + sub
            sector = block // BANDS
            band = block % BANDS
            mean = total[sub * BLOCK : (sub + 1) * BLOCK] * inverse[:, block : block + 1]
            static = jnp.concatenate(
                [
                    grid_ref[band * 8 + r, sector * 8 : sector * 8 + 8, :].astype(F32)
                    for r in range(8)
                ],
                axis=0,
            )
            hidden = mean + static
            hidden_ref[block * BLOCK : (block + 1) * BLOCK, :] = hidden
            store_normed(block * BLOCK, norm_rows(hidden, gain), normed_ref, west_ref, east_ref)


def combine(got, w_embed, grid_feat, gains):
    return pl.pallas_call(
        combine_kernel,
        out_shape=(pltpu.VMEM((CELLS, D), F32),) + NORMED_SHAPES,
        in_specs=[VMEM, HBM, HBM, VMEM],
        out_specs=(VMEM,) * 4,
        scratch_shapes=[
            pltpu.VMEM((SLOTS, D), BF16),
            pltpu.VMEM((DEVICES * 8, 128), F32),
            pltpu.VMEM((CELLS, SLOTS), BF16),
            pltpu.VMEM((FIN, D), BF16),
            pltpu.VMEM((16, 64, D), BF16),
            pltpu.SemaphoreType.DMA((2,)),
        ],
        compiler_params=PARAMS,
        name="combine",
    )(got, w_embed, grid_feat, gains)


def head_pair(query):
    lane = iota(query.shape, 1) < BLOCK
    zero = jnp.zeros_like(query)
    return jnp.concatenate([jnp.where(lane, query, zero), jnp.where(lane, zero, query)], axis=0)


def fold(values, op):
    rows, width = values.shape
    part = op(values.reshape(rows // BLOCK, BLOCK, width), axis=0)
    part = op(part.reshape(8, 8, width), axis=0)
    return op(part, axis=0, keepdims=True)


def soft(scores):
    highest = fold(scores, jnp.max)
    expo = jnp.exp(scores - highest)
    return expo.astype(BF16), highest, fold(expo, jnp.sum)


def staged(units, stages):
    held = {}
    for turn in range(len(units) + len(stages) - 1):
        for number, stage in enumerate(stages):
            at = turn - number
            if 0 <= at < len(units):
                held[at] = stage(units[at], held.get(at))


def near_columns(columns, query_ref, mixed_ref, highest_ref, total_ref):
    units = [(sector, pair) for sector in columns for pair in range(PAIRS)]

    def scored(unit, _):
        sector, pair = unit
        feats = slice(pair * 128, pair * 128 + 128)
        query = head_pair(query_ref[sector * COLUMN : (sector + 1) * COLUMN, feats])
        return lax.dot_general(columns[sector][0](feats), query, NT, preferred_element_type=F32)

    def weighed(unit, scores):
        return soft(scores)

    def summed(unit, held):
        sector, pair = unit
        weights, highest, total = held
        feats = slice(pair * 128, pair * 128 + 128)
        mixed = jnp.dot(columns[sector][1](feats), weights, preferred_element_type=F32)
        at = slice(sector * COLUMN, (sector + 1) * COLUMN)
        for h in range(2):
            head = pair * 2 + h
            lanes = slice(h * COLUMN, (h + 1) * COLUMN)
            mixed_ref[head * BLOCK : (head + 1) * BLOCK, at] = mixed[h * BLOCK : (h + 1) * BLOCK, lanes]
            highest_ref[head : head + 1, at] = highest[:, lanes]
            total_ref[head : head + 1, at] = total[:, lanes]

    staged(units, (scored, weighed, summed))


def inner_column(sector, key_ref, value_ref):
    at = slice((sector - 1) * COLUMN, (sector + 2) * COLUMN)
    return (lambda feats: key_ref[at, feats], lambda feats: value_ref[feats, at])


NEAR_SHAPES = (
    pltpu.VMEM((D, CELLS), F32),
    pltpu.VMEM((HEADS, CELLS), F32),
    pltpu.VMEM((HEADS, CELLS), F32),
)


def project_kernel(
    normed_ref, query_w, key_w, value_w,
    query_ref, key_ref, value_ref, mixed_ref, highest_ref, total_ref,
):
    flat = normed_ref[...]
    query = jnp.dot(flat, query_w[...], preferred_element_type=F32).astype(BF16)
    query_ref[...] = query * BF16(0.125)
    key_ref[...] = jnp.dot(flat, key_w[...], preferred_element_type=F32).astype(BF16)
    value_ref[...] = lax.dot_general(value_w[...], flat, NT, preferred_element_type=F32).astype(BF16)
    columns = {sector: inner_column(sector, key_ref, value_ref) for sector in range(1, EARLY)}
    near_columns(columns, query_ref, mixed_ref, highest_ref, total_ref)


def project(normed, w_query, w_key, w_value):
    shape = pltpu.VMEM((CELLS, D), BF16)
    return pl.pallas_call(
        project_kernel,
        out_shape=(shape, shape, pltpu.VMEM((D, CELLS), BF16)) + NEAR_SHAPES,
        in_specs=[VMEM] * 4,
        out_specs=(VMEM,) * 6,
        compiler_params=PARAMS,
        cost_estimate=pl.CostEstimate(flops=6 * CELLS * D * D, transcendentals=0, bytes_accessed=5 << 20),
        name="project",
    )(normed, w_query, w_key, w_value)


def margins_kernel(normed_ref, west_ref, east_ref, top_ref, low_ref):
    for band, out in enumerate((top_ref, low_ref)):
        here = slice(band * BLOCK, (band + 1) * BLOCK)
        out[0:BLOCK, :] = west_ref[here, :]
        for sector in range(SECTORS):
            at = (sector * BANDS + band) * BLOCK
            out[(sector + 1) * BLOCK : (sector + 2) * BLOCK, :] = normed_ref[at : at + BLOCK, :]
        out[BLOCK + HALO : WIDE, :] = east_ref[here, :]


def margins(normed, west, east):
    shape = pltpu.VMEM((WIDE, D), BF16)
    return pl.pallas_call(
        margins_kernel,
        out_shape=(shape, shape),
        in_specs=[VMEM] * 3,
        out_specs=(VMEM,) * 2,
        compiler_params=PARAMS,
        name="margins",
    )(normed, west, east)


def near_kernel(
    query_ref, key_ref, value_ref, west_ref, east_ref, key_w, value_w, mixed_in, highest_in, total_in,
    mixed_ref, highest_ref, total_ref,
):
    del mixed_in, highest_in, total_in
    outs = (query_ref, mixed_ref, highest_ref, total_ref)
    sides = jnp.concatenate([west_ref[...], east_ref[...]], axis=0)
    side_keys = jnp.dot(sides, key_w[...], preferred_element_type=F32).astype(BF16)
    side_values = lax.dot_general(value_w[...], sides, NT, preferred_element_type=F32).astype(BF16)
    columns = {
        sector: inner_column(sector, key_ref, value_ref) for sector in range(EARLY, SECTORS - 1)
    }
    inner = 2 * COLUMN
    columns[0] = (
        lambda feats: jnp.concatenate([side_keys[:COLUMN, feats], key_ref[:inner, feats]], axis=0),
        lambda feats: jnp.concatenate(
            [side_values[feats, :COLUMN], value_ref[feats, :inner]], axis=1
        ),
    )
    columns[SECTORS - 1] = (
        lambda feats: jnp.concatenate(
            [key_ref[CELLS - inner :, feats], side_keys[COLUMN:, feats]], axis=0
        ),
        lambda feats: jnp.concatenate(
            [value_ref[feats, CELLS - inner :], side_values[feats, COLUMN:]], axis=1
        ),
    )
    near_columns(columns, *outs)


def near(query, key, value, west, east, w_key, w_value, parts):
    return pl.pallas_call(
        near_kernel,
        out_shape=NEAR_SHAPES,
        in_specs=[VMEM] * 10,
        out_specs=(VMEM,) * 3,
        input_output_aliases={7: 0, 8: 1, 9: 2},
        compiler_params=PARAMS,
        cost_estimate=pl.CostEstimate(flops=8 << 30, transcendentals=4 << 20, bytes_accessed=8 << 20),
        name="near",
    )(query, key, value, west, east, w_key, w_value, *parts)


def make_far_kernel(last):
    def far_kernel(
        lat_ref, query_ref, mixed_ref, highest_ref, total_ref, up_ref, down_ref,
        hidden_ref, gain_ref, key_w, value_w, out_w, *rest,
    ):
        if last:
            out_ref, key_f, value_f, att_ref, new_ref = rest
        else:
            new_ref, normed_ref, west_ref, east_ref, key_f, value_f, att_ref = rest
        for band, source in enumerate((up_ref, down_ref)):
            rows = source[...]
            key_f[band] = jnp.dot(rows, key_w[...], preferred_element_type=F32).astype(BF16)
            value_f[band] = lax.dot_general(
                value_w[...], rows, NT, preferred_element_type=F32
            ).astype(BF16)
        beyond = (lat_ref[0] == 0, lat_ref[0] == lat_ref[1] - 1)
        span = 4 * BLOCK

        def hide(scores):
            second = iota((BLOCK, 2 * COLUMN), 1) % COLUMN >= BLOCK
            return jnp.concatenate(
                [
                    jnp.where(second, NEG, scores[:BLOCK]),
                    scores[BLOCK : 3 * BLOCK],
                    jnp.where(second, scores[3 * BLOCK :], NEG),
                ],
                axis=0,
            )

        def scored(unit, _):
            step, pair, band = unit
            feats = slice(pair * 128, pair * 128 + 128)
            first = step * 2 * COLUMN + band * BLOCK
            query = jnp.concatenate(
                [
                    query_ref[first : first + BLOCK, feats],
                    query_ref[first + COLUMN : first + COLUMN + BLOCK, feats],
                ],
                axis=0,
            )
            keys = key_f[band, step * COLUMN : step * COLUMN + span, feats]
            return hide(lax.dot_general(keys, head_pair(query), NT, preferred_element_type=F32))

        def weighed(unit, scores):
            return soft(scores)

        def summed(unit, held):
            step, pair, band = unit
            weights, highest, total = held
            feats = slice(pair * 128, pair * 128 + 128)
            values = value_f[band, feats, step * COLUMN : step * COLUMN + span]
            mixed = jnp.dot(values, weights, preferred_element_type=F32)
            waiting[unit] = (mixed, jnp.where(beyond[band], NEG, highest), total)
            if band == 1:
                merge(step, pair, waiting.pop((step, pair, 0)), waiting.pop(unit))

        def merge(step, pair, upper, lower):
            for h in range(2):
                head = pair * 2 + h
                rows = slice(head * BLOCK, (head + 1) * BLOCK)
                lanes = slice(h * COLUMN, (h + 1) * COLUMN)
                here = slice(h * BLOCK, (h + 1) * BLOCK)
                for second in range(2):
                    moved = []
                    for which in range(3):
                        x = upper[which][here if which == 0 else slice(None), lanes]
                        y = lower[which][here if which == 0 else slice(None), lanes]
                        if second:
                            x = pltpu.roll(x, BLOCK, 1)
                        else:
                            y = pltpu.roll(y, BLOCK, 1)
                        moved.append(jnp.where(iota(x.shape, 1) < BLOCK, x, y))
                    mixed, highest, total = moved
                    cells = slice((step * 2 + second) * COLUMN, (step * 2 + second + 1) * COLUMN)
                    highest_near = highest_ref[head : head + 1, cells]
                    top = jnp.maximum(highest, highest_near)
                    near_part = jnp.exp(highest_near - top)
                    far_part = jnp.exp(highest - top)
                    weight = total_ref[head : head + 1, cells] * near_part + total * far_part
                    near_part = near_part / weight
                    far_part = far_part / weight
                    att_ref[rows, cells] = (
                        mixed_ref[rows, cells] * near_part + mixed * far_part
                    ).astype(BF16)

        waiting = {}
        staged(
            [
                (step, pair, band)
                for step in range(SECTORS // 2)
                for pair in range(PAIRS)
                for band in range(BANDS)
            ],
            (scored, weighed, summed),
        )
        gain = gain_ref[...]
        for at in range(0, CELLS, 256):
            update = lax.dot_general(
                att_ref[:, at : at + 256], out_w[...], TN, preferred_element_type=F32
            )
            hidden = hidden_ref[at : at + 256, :] + update
            new_ref[at : at + 256, :] = hidden
            if not last:
                store_normed(at, norm_rows(hidden, gain), normed_ref, west_ref, east_ref)
        if last:
            for band in range(BANDS):
                for r in range(8):
                    pieces = []
                    for sector in range(SECTORS):
                        at = (sector * BANDS + band) * BLOCK + r * 8
                        pieces.append(new_ref[at : at + 8, :])
                    out_ref[band * 8 + r] = jnp.concatenate(pieces, axis=0).astype(BF16)

    return far_kernel


def far(place, query, parts, up, down, hidden, gain, w_key, w_value, w_out, last):
    scratch = [
        pltpu.VMEM((BANDS, WIDE, D), BF16),
        pltpu.VMEM((BANDS, D, WIDE), BF16),
        pltpu.VMEM((D, CELLS), BF16),
    ]
    if last:
        scratch.append(pltpu.VMEM((CELLS, D), F32))
        out_shape = jax.ShapeDtypeStruct((16, 64, D), BF16)
        out_specs = VMEM
    else:
        out_shape = (pltpu.VMEM((CELLS, D), F32),) + NORMED_SHAPES
        out_specs = (VMEM,) * 4
    return pl.pallas_call(
        make_far_kernel(last),
        out_shape=out_shape,
        in_specs=[SMEM] + [VMEM] * 11,
        out_specs=out_specs,
        scratch_shapes=scratch,
        compiler_params=PARAMS,
        name="far",
    )(place, query, *parts, up, down, hidden, gain, w_key, w_value, w_out)


def local(
    obs_feat, obs_owner, obs_cell, obs_valid, grid_feat,
    w_embed, gains, w_query, w_key, w_value, w_out,
):
    send = dispatch(
        obs_owner.reshape(1, OBS), obs_cell.reshape(1, OBS), obs_valid.reshape(1, OBS), off_chip(obs_feat)
    )
    got = lax.all_to_all(send, ("lat", "lon"), split_axis=0, concat_axis=0, tiled=True)
    hidden, normed, western, eastern = combine(got, off_chip(w_embed), off_chip(grid_feat), gains)
    lat_count = lax.axis_size("lat")
    lon_count = lax.axis_size("lon")
    place = jnp.stack([lax.axis_index("lat"), jnp.int32(lat_count)])
    rising = [(i, i + 1) for i in range(lat_count - 1)]
    falling = [(b, a) for a, b in rising]
    forward = [(i, (i + 1) % lon_count) for i in range(lon_count)]
    backward = [(b, a) for a, b in forward]
    for layer in range(LAYERS):
        last = layer == LAYERS - 1
        key_w = on_chip(w_key[layer])
        value_w = on_chip(jnp.transpose(w_value[layer]))
        hidden = on_chip(hidden)
        normed = on_chip(normed)
        west = lax.ppermute(on_chip(eastern), "lon", forward)
        east = lax.ppermute(on_chip(western), "lon", backward)
        query, key, value, *parts = project(normed, on_chip(w_query[layer]), key_w, value_w)
        query = on_chip(query)
        top, low = margins(normed, west, east)
        up = lax.ppermute(on_chip(low), "lat", rising)
        down = lax.ppermute(on_chip(top), "lat", falling)
        parts = [on_chip(part) for part in parts]
        parts = near(query, on_chip(key), on_chip(value), west, east, key_w, value_w, parts)
        following = min(layer + 1, LAYERS - 1)
        result = far(
            place, query, [on_chip(part) for part in parts], up, down, hidden,
            gains[following : following + 1], key_w, value_w, on_chip(w_out[layer]), last,
        )
        if not last:
            hidden, normed, western, eastern = result
    return result


def solution(mesh):
    placed = (
        P(("lat", "lon"), None),
        P(("lat", "lon"), None),
        P(("lat", "lon")),
        P(("lat", "lon")),
        P("lat", "lon", None),
        P(), P(), P(), P(), P(), P(),
    )
    return jax.shard_map(
        local, mesh=mesh, in_specs=placed, out_specs=P("lat", "lon", None), check_vma=False
    )
```

```python
import jax
import jax.numpy as jnp
from jax import lax
from jax.experimental import pallas as pl
from jax.experimental.pallas import tpu as pltpu
from jax.sharding import PartitionSpec as P

HEADS = 8
LAYERS = 2
D = 512
FIN = 256
DEVICES = 128
CAP = 16
ROWS = 40
OBS = 1024
CELLS = 1024
SLOTS = DEVICES * CAP
BLOCK = 64
BANDS = 2
SECTORS = 8
FRAME = SECTORS + 2
PAIRS = HEADS // 2
COLUMN = BANDS * BLOCK
NEG = -1e30
F32 = jnp.float32
BF16 = jnp.bfloat16

VMEM = pl.BlockSpec(memory_space=pltpu.VMEM)
SMEM = pl.BlockSpec(memory_space=pltpu.SMEM)
HBM = pl.BlockSpec(memory_space=pl.ANY)
PARAMS = pltpu.CompilerParams(vmem_limit_bytes=40 * 1024 * 1024)
WIDE = FRAME * BLOCK
HALO = SECTORS * BLOCK
NT = (((1,), (1,)), ((), ()))
TN = (((0,), (0,)), ((), ()))


def iota(shape, axis):
    return lax.broadcasted_iota(jnp.int32, shape, axis)


def dispatch_kernel(
    owner_hbm, cell_hbm, valid_hbm, feat_hbm, send_ref, owner_ref, cell_ref, valid_ref, feat_ref, sems
):
    pairs = ((owner_hbm, owner_ref), (cell_hbm, cell_ref), (valid_hbm, valid_ref), (feat_hbm, feat_ref))
    copies = [pltpu.make_async_copy(a, b, sems.at[i]) for i, (a, b) in enumerate(pairs)]
    for copy in copies:
        copy.start()
    for copy in copies[:3]:
        copy.wait()
    owner = owner_ref[...]
    cell = cell_ref[...]
    valid = valid_ref[...]
    wide = 256
    earlier = (iota((wide, wide), 0) < iota((wide, wide), 1)).astype(F32).astype(BF16)
    carry = jnp.zeros((DEVICES, 1), F32)
    ranks = []
    chosen = []
    for at in range(0, OBS, wide):
        hot = (iota((DEVICES, wide), 0) == owner[:, at : at + wide]).astype(F32)
        before = jnp.dot(hot.astype(BF16), earlier, preferred_element_type=F32) + carry
        ranks.append(jnp.sum(hot * before, axis=0, keepdims=True))
        carry = carry + jnp.sum(hot, axis=1, keepdims=True)
        chosen.append(hot.astype(BF16))
    rank = jnp.concatenate(ranks, axis=1).astype(jnp.int32)
    hot_all = jnp.concatenate(chosen, axis=1)
    row = cell // 64
    col = cell % 64
    high = (col // 8) * BANDS + row // 8 + 1
    low = (row % 8) * 8 + col % 8
    usable = valid == 1
    high = jnp.where(usable, high, 0)
    low = jnp.where(usable, low, 0)
    lane = iota((128, OBS), 0)
    part = jnp.where(lane < CAP, high, jnp.where(lane < 2 * CAP, low, 0))
    entry = jnp.where(lane % CAP == rank, part, 0).astype(F32).astype(BF16)
    tags = lax.dot_general(hot_all, entry, NT, preferred_element_type=F32)
    send_ref[:, 32:40, :] = jnp.broadcast_to(tags[:, None, :], (DEVICES, 8, 128)).astype(BF16)
    target = owner * CAP + rank
    copies[3].wait()
    feat = feat_ref[...]
    step = 256
    for at in range(0, SLOTS, step):
        pick = (iota((step, OBS), 0) + at == target).astype(F32).astype(BF16)
        rows = jnp.dot(pick, feat, preferred_element_type=F32).astype(BF16)
        first = at // CAP
        count = step // CAP
        send_ref[first : first + count, 0:16, :] = rows[:, :128].reshape(count, CAP, 128)
        send_ref[first : first + count, 16:32, :] = rows[:, 128:].reshape(count, CAP, 128)


def dispatch(owner, cell, valid, feat):
    return pl.pallas_call(
        dispatch_kernel,
        out_shape=jax.ShapeDtypeStruct((DEVICES, ROWS, 128), BF16),
        in_specs=[HBM] * 4,
        out_specs=VMEM,
        scratch_shapes=[pltpu.VMEM((1, OBS), jnp.int32)] * 3
        + [pltpu.VMEM((OBS, FIN), BF16), pltpu.SemaphoreType.DMA((4,))],
        compiler_params=PARAMS,
        name="dispatch",
    )(owner, cell, valid, feat)


def on_chip(array):
    return pltpu.with_memory_space_constraint(array, pltpu.VMEM)


def off_chip(array):
    return pltpu.with_memory_space_constraint(array, pltpu.HBM)


def norm_rows(hidden, gain):
    scale = lax.rsqrt(jnp.mean(hidden * hidden, axis=-1, keepdims=True) + 1e-06)
    return (hidden * scale * gain).astype(BF16)


def pick(choose, x, y):
    return jnp.where(choose, x, y)


def store_normed(sector, rows, refs, place_ref):
    normed_ref, first_ref, second_ref, third_ref, fourth_ref = refs
    here = slice(sector * BLOCK, (sector + 1) * BLOCK)
    normed_ref[sector * COLUMN : (sector + 1) * COLUMN, :] = rows
    even = place_ref[2] == 0
    top = rows[:BLOCK]
    low = rows[BLOCK:]
    first_ref[here, :] = pick(even, low, top)
    second_ref[here, :] = pick(even, top, low)
    if sector == 0:
        third_ref[...] = rows
        fourth_ref[...] = rows
    if sector == SECTORS - 1:
        even = place_ref[3] == 0
        third_ref[...] = pick(even, rows, third_ref[...])
        fourth_ref[...] = pick(even, fourth_ref[...], rows)


NORMED_SHAPES = (
    pltpu.VMEM((CELLS, D), BF16),
    pltpu.VMEM((HALO, D), BF16),
    pltpu.VMEM((HALO, D), BF16),
    pltpu.VMEM((COLUMN, D), BF16),
    pltpu.VMEM((COLUMN, D), BF16),
)


def gelu(x):
    inner = x * (0.7978845608028654 + (0.7978845608028654 * 0.044715) * (x * x))
    half = 0.5 * x
    return half + half * jnp.tanh(inner)


def combine_kernel(
    place_ref, got_ref, embed_hbm, grid_hbm, gain_ref, hidden_ref, *rest
):
    refs = rest[:5]
    emb_ref, tag_ref, hot_ref, embed_ref, grid_ref, sems = rest[5:]
    fetch_embed = pltpu.make_async_copy(embed_hbm, embed_ref, sems.at[0])
    fetch_grid = pltpu.make_async_copy(grid_hbm, grid_ref, sems.at[1])
    fetch_embed.start()
    fetch_grid.start()
    tag_ref[...] = got_ref[:, 32:40, :].astype(F32).reshape(DEVICES * 8, 128)
    tags = tag_ref[pl.ds(0, DEVICES, stride=8), :]
    tags = jnp.transpose(tags)[: 2 * CAP].astype(BF16)
    spread = (iota((DEVICES, SLOTS), 1) // CAP == iota((DEVICES, SLOTS), 0)).astype(F32).astype(BF16)
    wide = jnp.dot(tags, spread, preferred_element_type=F32)
    own = iota((CAP, SLOTS), 1) % CAP == iota((CAP, SLOTS), 0)
    high = jnp.sum(jnp.where(own, wide[:CAP], 0.0), axis=0, keepdims=True)
    low = jnp.sum(jnp.where(own, wide[CAP:], 0.0), axis=0, keepdims=True)
    low_hot = (iota((BLOCK, SLOTS), 0).astype(F32) == low).astype(F32).astype(BF16)
    high_hot = (iota((16, SLOTS), 0).astype(F32) + 1.0 == high).astype(F32).astype(BF16)
    counts = lax.dot_general(low_hot, high_hot, NT, preferred_element_type=F32)
    inverse = 1.0 / jnp.maximum(counts, 1.0)
    high16 = jnp.broadcast_to(high, (16, SLOTS))
    for block in range(BANDS * SECTORS):
        mask = (high16 == block + 1.0).astype(F32).astype(BF16)
        for part in range(BLOCK // 16):
            at = block * BLOCK + part * 16
            hot_ref[at : at + 16, :] = low_hot[part * 16 : part * 16 + 16] * mask
    fetch_embed.wait()
    step = 512
    for at in range(0, SLOTS, step):
        first = at // CAP
        count = step // CAP
        left = got_ref[first : first + count, 0:16, :].reshape(step, 128)
        right = got_ref[first : first + count, 16:32, :].reshape(step, 128)
        raw = jnp.concatenate([left, right], axis=1)
        product = jnp.dot(raw, embed_ref[...], preferred_element_type=F32)
        emb_ref[at : at + step, :] = gelu(product).astype(BF16)
    gain = gain_ref[0:1, :]
    fetch_grid.wait()
    chunk = 512
    for start in range(0, CELLS, chunk):
        total = jnp.dot(hot_ref[start : start + chunk, :], emb_ref[...], preferred_element_type=F32)
        for sub in range(chunk // COLUMN):
            sector = start // COLUMN + sub
            pieces = []
            for band in range(BANDS):
                block = sector * BANDS + band
                row = sub * COLUMN + band * BLOCK
                mean = total[row : row + BLOCK] * inverse[:, block : block + 1]
                static = jnp.concatenate(
                    [
                        grid_ref[band * 8 + r, sector * 8 : sector * 8 + 8, :].astype(F32)
                        for r in range(8)
                    ],
                    axis=0,
                )
                pieces.append(mean + static)
            hidden = jnp.concatenate(pieces, axis=0)
            hidden_ref[sector * COLUMN : (sector + 1) * COLUMN, :] = hidden
            store_normed(sector, norm_rows(hidden, gain), refs, place_ref)


def combine(place, got, w_embed, grid_feat, gains):
    return pl.pallas_call(
        combine_kernel,
        out_shape=(pltpu.VMEM((CELLS, D), F32),) + NORMED_SHAPES,
        in_specs=[SMEM, VMEM, HBM, HBM, VMEM],
        out_specs=(VMEM,) * 6,
        scratch_shapes=[
            pltpu.VMEM((SLOTS, D), BF16),
            pltpu.VMEM((DEVICES * 8, 128), F32),
            pltpu.VMEM((CELLS, SLOTS), BF16),
            pltpu.VMEM((FIN, D), BF16),
            pltpu.VMEM((16, 64, D), BF16),
            pltpu.SemaphoreType.DMA((2,)),
        ],
        compiler_params=PARAMS,
        name="combine",
    )(place, got, w_embed, grid_feat, gains)


def head_pair(query):
    lane = iota(query.shape, 1) < BLOCK
    zero = jnp.zeros_like(query)
    return jnp.concatenate([jnp.where(lane, query, zero), jnp.where(lane, zero, query)], axis=0)


def fold(values, op):
    rows, width = values.shape
    part = op(values.reshape(rows // BLOCK, BLOCK, width), axis=0)
    part = op(part.reshape(8, 8, width), axis=0)
    return op(part, axis=0, keepdims=True)


def soft(scores):
    highest = fold(scores, jnp.max)
    expo = jnp.exp(scores - highest)
    return expo.astype(BF16), highest, fold(expo, jnp.sum)


def staged(units, stages):
    held = {}
    for turn in range(len(units) + len(stages) - 1):
        for number, stage in enumerate(stages):
            at = turn - number
            if 0 <= at < len(units):
                held[at] = stage(units[at], held.get(at))


def near_columns(columns, query_ref, mixed_ref, highest_ref, total_ref):
    units = [(sector, pair) for sector in columns for pair in range(PAIRS)]

    def scored(unit, _):
        sector, pair = unit
        feats = slice(pair * 128, pair * 128 + 128)
        query = head_pair(query_ref[sector * COLUMN : (sector + 1) * COLUMN, feats])
        return lax.dot_general(columns[sector][0](feats), query, NT, preferred_element_type=F32)

    def weighed(unit, scores):
        return soft(scores)

    def summed(unit, held):
        sector, pair = unit
        weights, highest, total = held
        feats = slice(pair * 128, pair * 128 + 128)
        mixed = jnp.dot(columns[sector][1](feats), weights, preferred_element_type=F32)
        at = slice(sector * COLUMN, (sector + 1) * COLUMN)
        for h in range(2):
            head = pair * 2 + h
            lanes = slice(h * COLUMN, (h + 1) * COLUMN)
            mixed_ref[head * BLOCK : (head + 1) * BLOCK, at] = mixed[h * BLOCK : (h + 1) * BLOCK, lanes]
            highest_ref[head : head + 1, at] = highest[:, lanes]
            total_ref[head : head + 1, at] = total[:, lanes]

    staged(units, (scored, weighed, summed))


def inner_column(sector, key_ref, value_ref):
    at = slice((sector - 1) * COLUMN, (sector + 2) * COLUMN)
    return (lambda feats: key_ref[at, feats], lambda feats: value_ref[feats, at])


NEAR_SHAPES = (
    pltpu.VMEM((D, CELLS), F32),
    pltpu.VMEM((HEADS, CELLS), F32),
    pltpu.VMEM((HEADS, CELLS), F32),
)


def project_kernel(
    normed_ref, query_w, key_w, value_w,
    query_ref, key_ref, value_ref, mixed_ref, highest_ref, total_ref,
):
    flat = normed_ref[...]
    query = jnp.dot(flat, query_w[...], preferred_element_type=F32).astype(BF16)
    query_ref[...] = query * BF16(0.125)
    key_ref[...] = jnp.dot(flat, key_w[...], preferred_element_type=F32).astype(BF16)
    value_ref[...] = lax.dot_general(value_w[...], flat, NT, preferred_element_type=F32).astype(BF16)
    columns = {sector: inner_column(sector, key_ref, value_ref) for sector in range(1, SECTORS - 1)}
    near_columns(columns, query_ref, mixed_ref, highest_ref, total_ref)


def project(normed, w_query, w_key, w_value):
    shape = pltpu.VMEM((CELLS, D), BF16)
    return pl.pallas_call(
        project_kernel,
        out_shape=(shape, shape, pltpu.VMEM((D, CELLS), BF16)) + NEAR_SHAPES,
        in_specs=[VMEM] * 4,
        out_specs=(VMEM,) * 6,
        compiler_params=PARAMS,
        cost_estimate=pl.CostEstimate(flops=6 * CELLS * D * D, transcendentals=0, bytes_accessed=5 << 20),
        name="project",
    )(normed, w_query, w_key, w_value)


def sides_of(place_ref, third_ref, fourth_ref):
    even = place_ref[3] == 0
    third = third_ref[...]
    fourth = fourth_ref[...]
    return pick(even, fourth, third), pick(even, third, fourth)


def rows_of(place_ref, first_ref, second_ref):
    even = place_ref[2] == 0
    first = first_ref[...]
    second = second_ref[...]
    return pick(even, second, first), pick(even, first, second)


def corners_kernel(place_ref, third_ref, fourth_ref, first_ref, second_ref):
    west, east = sides_of(place_ref, third_ref, fourth_ref)
    even = place_ref[2] == 0
    top = jnp.concatenate([west[:BLOCK], east[:BLOCK]], axis=0)
    low = jnp.concatenate([west[BLOCK:], east[BLOCK:]], axis=0)
    first_ref[...] = pick(even, low, top)
    second_ref[...] = pick(even, top, low)


def corners(place, third, fourth):
    shape = pltpu.VMEM((COLUMN, D), BF16)
    return pl.pallas_call(
        corners_kernel,
        out_shape=(shape, shape),
        in_specs=[SMEM] + [VMEM] * 2,
        out_specs=(VMEM,) * 2,
        compiler_params=PARAMS,
        name="corners",
    )(place, third, fourth)


def near_kernel(
    place_ref, query_ref, key_ref, value_ref, third_ref, fourth_ref, key_w, value_w, mixed_in, highest_in, total_in,
    mixed_ref, highest_ref, total_ref,
):
    del mixed_in, highest_in, total_in
    outs = (query_ref, mixed_ref, highest_ref, total_ref)
    sides = jnp.concatenate(sides_of(place_ref, third_ref, fourth_ref), axis=0)
    side_keys = jnp.dot(sides, key_w[...], preferred_element_type=F32).astype(BF16)
    side_values = lax.dot_general(value_w[...], sides, NT, preferred_element_type=F32).astype(BF16)
    columns = {}
    inner = 2 * COLUMN
    columns[0] = (
        lambda feats: jnp.concatenate([side_keys[:COLUMN, feats], key_ref[:inner, feats]], axis=0),
        lambda feats: jnp.concatenate(
            [side_values[feats, :COLUMN], value_ref[feats, :inner]], axis=1
        ),
    )
    columns[SECTORS - 1] = (
        lambda feats: jnp.concatenate(
            [key_ref[CELLS - inner :, feats], side_keys[COLUMN:, feats]], axis=0
        ),
        lambda feats: jnp.concatenate(
            [value_ref[feats, CELLS - inner :], side_values[feats, COLUMN:]], axis=1
        ),
    )
    near_columns(columns, *outs)


def near(place, query, key, value, third, fourth, w_key, w_value, parts):
    return pl.pallas_call(
        near_kernel,
        out_shape=NEAR_SHAPES,
        in_specs=[SMEM] + [VMEM] * 10,
        out_specs=(VMEM,) * 3,
        input_output_aliases={8: 0, 9: 1, 10: 2},
        compiler_params=PARAMS,
        cost_estimate=pl.CostEstimate(flops=8 << 30, transcendentals=4 << 20, bytes_accessed=8 << 20),
        name="near",
    )(place, query, key, value, third, fourth, w_key, w_value, *parts)


def merge(tiles, head, cells, near_refs, store):
    mixed_ref, highest_ref, total_ref = near_refs
    mixed, highest, total = tiles
    rows = slice(head * BLOCK, (head + 1) * BLOCK)
    highest_near = highest_ref[head : head + 1, cells]
    top = jnp.maximum(highest, highest_near)
    near_part = jnp.exp(highest_near - top)
    far_part = jnp.exp(highest - top)
    weight = total_ref[head : head + 1, cells] * near_part + total * far_part
    near_part = near_part / weight
    far_part = far_part / weight
    store(rows, (mixed_ref[rows, cells] * near_part + mixed * far_part).astype(BF16))


def join(x, y, turn_x):
    if turn_x:
        x = pltpu.roll(x, BLOCK, 1)
    else:
        y = pltpu.roll(y, BLOCK, 1)
    return jnp.where(iota(x.shape, 1) < BLOCK, x, y)


def beyond_grid(place_ref):
    return (place_ref[0] == 0, place_ref[0] == place_ref[1] - 1)


def make_far_kernel(last):
    def far_kernel(
        place_ref, query_ref, mixed_ref, highest_ref, total_ref, first_ref, second_ref,
        hidden_ref, gain_ref, key_w, value_w, out_w, *rest,
    ):
        new_ref, key_f, value_f = rest[:3]
        refs = rest[3:-1]
        att_ref = rest[-1]
        near_refs = (mixed_ref, highest_ref, total_ref)
        for band, rows in enumerate(rows_of(place_ref, first_ref, second_ref)):
            key_f[band] = jnp.dot(rows, key_w[...], preferred_element_type=F32).astype(BF16)
            value_f[band] = lax.dot_general(
                value_w[...], rows, NT, preferred_element_type=F32
            ).astype(BF16)
        beyond = beyond_grid(place_ref)
        span = 4 * BLOCK

        def hide(scores):
            second = iota((BLOCK, 2 * COLUMN), 1) % COLUMN >= BLOCK
            return jnp.concatenate(
                [
                    jnp.where(second, NEG, scores[:BLOCK]),
                    scores[BLOCK : 3 * BLOCK],
                    jnp.where(second, scores[3 * BLOCK :], NEG),
                ],
                axis=0,
            )

        def scored(unit, _):
            step, pair, band = unit
            feats = slice(pair * 128, pair * 128 + 128)
            first = (step * 2 + 1) * COLUMN + band * BLOCK
            query = jnp.concatenate(
                [
                    query_ref[first : first + BLOCK, feats],
                    query_ref[first + COLUMN : first + COLUMN + BLOCK, feats],
                ],
                axis=0,
            )
            keys = key_f[band, step * COLUMN : step * COLUMN + span, feats]
            return hide(lax.dot_general(keys, head_pair(query), NT, preferred_element_type=F32))

        def weighed(unit, scores):
            return soft(scores)

        def summed(unit, held):
            step, pair, band = unit
            weights, highest, total = held
            feats = slice(pair * 128, pair * 128 + 128)
            values = value_f[band, feats, step * COLUMN : step * COLUMN + span]
            mixed = jnp.dot(values, weights, preferred_element_type=F32)
            waiting[unit] = (mixed, jnp.where(beyond[band], NEG, highest), total)
            if band == 0:
                return
            upper = waiting.pop((step, pair, 0))
            lower = waiting.pop(unit)
            for h in range(2):
                lanes = slice(h * COLUMN, (h + 1) * COLUMN)
                here = (slice(h * BLOCK, (h + 1) * BLOCK), slice(None), slice(None))
                for second in range(2):
                    tiles = [
                        join(x[part, lanes], y[part, lanes], second == 1)
                        for x, y, part in zip(upper, lower, here)
                    ]
                    at = (step * 2 + 1 + second) * COLUMN
                    cells = slice(at, at + COLUMN)

                    def store(rows, value):
                        att_ref[rows, cells] = value

                    merge(tiles, pair * 2 + h, cells, near_refs, store)

        waiting = {}
        staged(
            [
                (step, pair, band)
                for step in range(SECTORS // 2 - 1)
                for pair in range(PAIRS)
                for band in range(BANDS)
            ],
            (scored, weighed, summed),
        )
        gain = gain_ref[...]
        for at in range(COLUMN, CELLS - COLUMN, 256):
            update = lax.dot_general(
                att_ref[:, at : at + 256], out_w[...], TN, preferred_element_type=F32
            )
            hidden = hidden_ref[at : at + 256, :] + update
            new_ref[at : at + 256, :] = hidden
            if not last:
                normed = norm_rows(hidden, gain)
                for sub in range(256 // COLUMN):
                    store_normed(
                        at // COLUMN + sub,
                        normed[sub * COLUMN : (sub + 1) * COLUMN],
                        refs + (None, None),
                        place_ref,
                    )

    return far_kernel


def far(place, query, parts, first, second, hidden, gain, w_key, w_value, w_out, last):
    out_shape = (
        pltpu.VMEM((CELLS, D), F32),
        pltpu.VMEM((BANDS, HALO, D), BF16),
        pltpu.VMEM((BANDS, D, HALO), BF16),
    )
    if not last:
        out_shape = out_shape + NORMED_SHAPES[:3]
    return pl.pallas_call(
        make_far_kernel(last),
        out_shape=out_shape,
        in_specs=[SMEM] + [VMEM] * 11,
        out_specs=(VMEM,) * len(out_shape),
        scratch_shapes=[pltpu.VMEM((D, CELLS), BF16)],
        compiler_params=PARAMS,
        cost_estimate=pl.CostEstimate(flops=8 << 30, transcendentals=4 << 20, bytes_accessed=8 << 20),
        name="far",
    )(place, query, *parts, first, second, hidden, gain, w_key, w_value, w_out)


def make_edge_kernel(last):
    def edge_kernel(
        place_ref, query_ref, mixed_ref, highest_ref, total_ref, first_ref, second_ref,
        hidden_ref, gain_ref, key_w, value_w, out_w, key_f, value_f, *rest,
    ):
        near_refs = (mixed_ref, highest_ref, total_ref)
        att_ref = rest[-1]
        if last:
            inner_ref, out_ref, edge_ref = rest[:3]
        else:
            new_ref = rest[4]
            refs = rest[5:10]
        rows = jnp.concatenate(rows_of(place_ref, first_ref, second_ref), axis=0)
        corner_keys = jnp.dot(rows, key_w[...], preferred_element_type=F32).astype(BF16)
        corner_values = lax.dot_general(
            value_w[...], rows, NT, preferred_element_type=F32
        ).astype(BF16)
        beyond = beyond_grid(place_ref)
        starts = (0, HALO - 2 * BLOCK)

        def scored(unit, _):
            side, pair, band = unit
            feats = slice(pair * 128, pair * 128 + 128)
            first = side * (SECTORS - 1) * COLUMN + band * BLOCK
            corner = (band * 2 + side) * BLOCK
            keys = jnp.concatenate(
                [
                    key_f[band, starts[side] : starts[side] + 2 * BLOCK, feats],
                    corner_keys[corner : corner + BLOCK, feats],
                ],
                axis=0,
            )
            query = head_pair(query_ref[first : first + BLOCK, feats])
            return lax.dot_general(keys, query, NT, preferred_element_type=F32)

        def weighed(unit, scores):
            return soft(scores)

        def summed(unit, held):
            side, pair, band = unit
            weights, highest, total = held
            feats = slice(pair * 128, pair * 128 + 128)
            corner = (band * 2 + side) * BLOCK
            values = jnp.concatenate(
                [
                    value_f[band, feats, starts[side] : starts[side] + 2 * BLOCK],
                    corner_values[feats, corner : corner + BLOCK],
                ],
                axis=1,
            )
            mixed = jnp.dot(values, weights, preferred_element_type=F32)
            waiting[unit] = (mixed, jnp.where(beyond[band], NEG, highest), total)
            if band == 0:
                return
            upper = waiting.pop((side, pair, 0))
            lower = waiting.pop(unit)
            for h in range(2):
                here = (slice(h * BLOCK, (h + 1) * BLOCK), slice(None), slice(None))
                tiles = [join(x[part], y[part], h == 1) for x, y, part in zip(upper, lower, here)]
                at = side * (SECTORS - 1) * COLUMN
                lanes = slice(side * COLUMN, (side + 1) * COLUMN)

                def store(rows, value):
                    att_ref[rows, lanes] = value

                merge(tiles, pair * 2 + h, slice(at, at + COLUMN), near_refs, store)

        waiting = {}
        staged(
            [
                (side, pair, band)
                for side in range(2)
                for pair in range(PAIRS)
                for band in range(BANDS)
            ],
            (scored, weighed, summed),
        )
        update = lax.dot_general(att_ref[...], out_w[...], TN, preferred_element_type=F32)
        gain = gain_ref[...]
        for side in range(2):
            at = side * (CELLS - COLUMN)
            hidden = hidden_ref[at : at + COLUMN, :] + update[side * COLUMN : (side + 1) * COLUMN]
            if last:
                edge_ref[side * COLUMN : (side + 1) * COLUMN, :] = hidden
                continue
            new_ref[at : at + COLUMN, :] = hidden
            normed = norm_rows(hidden, gain)
            store_normed(at // COLUMN, normed, refs, place_ref)
        if last:
            for band in range(BANDS):
                for r in range(8):
                    pieces = []
                    for sector in range(SECTORS):
                        at = (sector * BANDS + band) * BLOCK + r * 8
                        if sector == 0:
                            pieces.append(edge_ref[at : at + 8, :])
                        elif sector == SECTORS - 1:
                            at = at - CELLS + 2 * COLUMN
                            pieces.append(edge_ref[at : at + 8, :])
                        else:
                            pieces.append(inner_ref[at : at + 8, :])
                    out_ref[band * 8 + r] = jnp.concatenate(pieces, axis=0).astype(BF16)

    return edge_kernel


def edges(place, query, parts, first, second, hidden, gain, w_key, w_value, w_out, inner, last):
    new, key_f, value_f, *normed = inner
    scratch = [pltpu.VMEM((D, 2 * COLUMN), BF16)]
    if last:
        scratch = [pltpu.VMEM((2 * COLUMN, D), F32)] + scratch
        out_shape = jax.ShapeDtypeStruct((16, 64, D), BF16)
        out_specs = VMEM
        aliases = {}
    else:
        out_shape = (pltpu.VMEM((CELLS, D), F32),) + NORMED_SHAPES
        out_specs = (VMEM,) * 6
        aliases = {14: 0, 15: 1, 16: 2, 17: 3}
    return pl.pallas_call(
        make_edge_kernel(last),
        out_shape=out_shape,
        in_specs=[SMEM] + [VMEM] * (14 + len(normed)),
        out_specs=out_specs,
        scratch_shapes=scratch,
        input_output_aliases=aliases,
        compiler_params=PARAMS,
        name="edges",
    )(place, query, *parts, first, second, hidden, gain, w_key, w_value, w_out, key_f, value_f, new, *normed)


def local(
    obs_feat, obs_owner, obs_cell, obs_valid, grid_feat,
    w_embed, gains, w_query, w_key, w_value, w_out,
):
    send = dispatch(
        off_chip(obs_owner.reshape(1, OBS)),
        off_chip(obs_cell.reshape(1, OBS)),
        off_chip(obs_valid.reshape(1, OBS)),
        off_chip(obs_feat),
    )
    got = lax.all_to_all(send, ("lat", "lon"), split_axis=0, concat_axis=0, tiled=True)
    lat_count = lax.axis_size("lat")
    lon_count = lax.axis_size("lon")
    lat = lax.axis_index("lat")
    lon = lax.axis_index("lon")
    place = jnp.stack([lat, jnp.int32(lat_count), lat % 2, lon % 2])
    hidden, *normed = combine(place, got, off_chip(w_embed), off_chip(grid_feat), gains)
    lat_first = [(i, i ^ 1) for i in range(lat_count)]
    lat_second = [(0, 0), (lat_count - 1, lat_count - 1)]
    for i in range(1, lat_count - 1, 2):
        lat_second += [(i, i + 1), (i + 1, i)]
    lon_first = [(i, i ^ 1) for i in range(lon_count)]
    lon_second = [(i, (((i + 1) ^ 1) - 1) % lon_count) for i in range(lon_count)]
    for layer in range(LAYERS):
        last = layer == LAYERS - 1
        key_w = on_chip(w_key[layer])
        value_w = on_chip(jnp.transpose(w_value[layer]))
        hidden = on_chip(hidden)
        flat, *trades = [on_chip(item) for item in normed]
        third = lax.ppermute(trades[2], "lon", lon_first)
        fourth = lax.ppermute(trades[3], "lon", lon_second)
        second = lax.ppermute(trades[1], "lat", lat_second)
        first = lax.ppermute(trades[0], "lat", lat_first)
        query, key, value, *parts = project(flat, on_chip(w_query[layer]), key_w, value_w)
        query = on_chip(query)
        corner = corners(place, third, fourth)
        corner_second = lax.ppermute(on_chip(corner[1]), "lat", lat_second)
        corner_first = lax.ppermute(on_chip(corner[0]), "lat", lat_first)
        parts = [on_chip(part) for part in parts]
        parts = near(
            place, query, on_chip(key), on_chip(value), third, fourth, key_w, value_w, parts
        )
        parts = [on_chip(part) for part in parts]
        following = min(layer + 1, LAYERS - 1)
        gain = gains[following : following + 1]
        out_w = on_chip(w_out[layer])
        inner = far(place, query, parts, first, second, hidden, gain, key_w, value_w, out_w, last)
        inner = [on_chip(item) for item in inner]
        result = edges(
            place, query, parts, corner_first, corner_second, hidden, gain, key_w, value_w, out_w, inner, last
        )
        if not last:
            hidden, *normed = result
    return result


def solution(mesh):
    placed = (
        P(("lat", "lon"), None),
        P(("lat", "lon"), None),
        P(("lat", "lon")),
        P(("lat", "lon")),
        P("lat", "lon", None),
        P(), P(), P(), P(), P(), P(),
    )
    return jax.shard_map(
        local, mesh=mesh, in_specs=placed, out_specs=P("lat", "lon", None), check_vma=False
    )
```

```python
import jax
import jax.numpy as jnp
from jax import lax
from jax.experimental import pallas as pl
from jax.experimental.pallas import tpu as pltpu
from jax.sharding import PartitionSpec as P

HEADS = 8
LAYERS = 2
D = 512
FIN = 256
DEVICES = 128
CAP = 16
ROWS = 40
OBS = 1024
CELLS = 1024
SLOTS = DEVICES * CAP
BLOCK = 64
BANDS = 2
SECTORS = 8
FRAME = SECTORS + 2
PAIRS = HEADS // 2
COLUMN = BANDS * BLOCK
NEG = -1e30
F32 = jnp.float32
BF16 = jnp.bfloat16

VMEM = pl.BlockSpec(memory_space=pltpu.VMEM)
HBM = pl.BlockSpec(memory_space=pl.ANY)
PARAMS = pltpu.CompilerParams(vmem_limit_bytes=40 * 1024 * 1024)
WIDE = FRAME * BLOCK
HALO = SECTORS * BLOCK
NT = (((1,), (1,)), ((), ()))
TN = (((0,), (0,)), ((), ()))


def iota(shape, axis):
    return lax.broadcasted_iota(jnp.int32, shape, axis)


def dispatch_kernel(
    owner_hbm, cell_hbm, valid_hbm, feat_hbm, send_ref, owner_ref, cell_ref, valid_ref, feat_ref, sems
):
    pairs = ((owner_hbm, owner_ref), (cell_hbm, cell_ref), (valid_hbm, valid_ref), (feat_hbm, feat_ref))
    copies = [pltpu.make_async_copy(a, b, sems.at[i]) for i, (a, b) in enumerate(pairs)]
    for copy in copies:
        copy.start()
    for copy in copies[:3]:
        copy.wait()
    owner = owner_ref[...]
    cell = cell_ref[...]
    valid = valid_ref[...]
    wide = 256
    earlier = (iota((wide, wide), 0) < iota((wide, wide), 1)).astype(F32).astype(BF16)
    carry = jnp.zeros((DEVICES, 1), F32)
    ranks = []
    chosen = []
    for at in range(0, OBS, wide):
        hot = (iota((DEVICES, wide), 0) == owner[:, at : at + wide]).astype(F32)
        before = jnp.dot(hot.astype(BF16), earlier, preferred_element_type=F32) + carry
        ranks.append(jnp.sum(hot * before, axis=0, keepdims=True))
        carry = carry + jnp.sum(hot, axis=1, keepdims=True)
        chosen.append(hot.astype(BF16))
    rank = jnp.concatenate(ranks, axis=1).astype(jnp.int32)
    hot_all = jnp.concatenate(chosen, axis=1)
    row = cell // 64
    col = cell % 64
    high = (col // 8) * BANDS + row // 8 + 1
    low = (row % 8) * 8 + col % 8
    usable = valid == 1
    high = jnp.where(usable, high, 0)
    low = jnp.where(usable, low, 0)
    lane = iota((128, OBS), 0)
    part = jnp.where(lane < CAP, high, jnp.where(lane < 2 * CAP, low, 0))
    entry = jnp.where(lane % CAP == rank, part, 0).astype(F32).astype(BF16)
    tags = lax.dot_general(hot_all, entry, NT, preferred_element_type=F32)
    send_ref[:, 32:40, :] = jnp.broadcast_to(tags[:, None, :], (DEVICES, 8, 128)).astype(BF16)
    target = owner * CAP + rank
    copies[3].wait()
    feat = feat_ref[...]
    step = 256
    for at in range(0, SLOTS, step):
        pick = (iota((step, OBS), 0) + at == target).astype(F32).astype(BF16)
        rows = jnp.dot(pick, feat, preferred_element_type=F32).astype(BF16)
        first = at // CAP
        count = step // CAP
        send_ref[first : first + count, 0:16, :] = rows[:, :128].reshape(count, CAP, 128)
        send_ref[first : first + count, 16:32, :] = rows[:, 128:].reshape(count, CAP, 128)


def dispatch(owner, cell, valid, feat):
    return pl.pallas_call(
        dispatch_kernel,
        out_shape=pltpu.VMEM((DEVICES, ROWS, 128), BF16),
        in_specs=[HBM] * 4,
        out_specs=VMEM,
        scratch_shapes=[pltpu.VMEM((1, OBS), jnp.int32)] * 3
        + [pltpu.VMEM((OBS, FIN), BF16), pltpu.SemaphoreType.DMA((4,))],
        compiler_params=PARAMS,
        name="dispatch",
    )(owner, cell, valid, feat)


def on_chip(array):
    return pltpu.with_memory_space_constraint(array, pltpu.VMEM)


def off_chip(array):
    return pltpu.with_memory_space_constraint(array, pltpu.HBM)


def norm_rows(hidden, gain):
    scale = lax.rsqrt(jnp.mean(hidden * hidden, axis=-1, keepdims=True) + 1e-06)
    return (hidden * scale * gain).astype(BF16)


def pick(choose, x, y):
    return jnp.where(choose, x, y)


def store_normed(sector, rows, refs):
    normed_ref, first_ref, second_ref, third_ref, fourth_ref = refs
    here = slice(sector * BLOCK, (sector + 1) * BLOCK)
    normed_ref[sector * COLUMN : (sector + 1) * COLUMN, :] = rows
    even = lax.axis_index("lat") % 2 == 0
    top = rows[:BLOCK]
    low = rows[BLOCK:]
    first_ref[here, :] = pick(even, low, top)
    second_ref[here, :] = pick(even, top, low)
    if sector == 0:
        third_ref[...] = rows
        fourth_ref[...] = rows
    if sector == SECTORS - 1:
        even = lax.axis_index("lon") % 2 == 0
        third_ref[...] = pick(even, rows, third_ref[...])
        fourth_ref[...] = pick(even, fourth_ref[...], rows)


NORMED_SHAPES = (
    pltpu.VMEM((CELLS, D), BF16),
    pltpu.VMEM((HALO, D), BF16),
    pltpu.VMEM((HALO, D), BF16),
    pltpu.VMEM((COLUMN, D), BF16),
    pltpu.VMEM((COLUMN, D), BF16),
)


def gelu(x):
    inner = x * (0.7978845608028654 + (0.7978845608028654 * 0.044715) * (x * x))
    half = 0.5 * x
    return half + half * jnp.tanh(inner)


def combine_kernel(
    got_ref, embed_hbm, grid_hbm, gain_ref, hidden_ref, *rest
):
    refs = rest[:5]
    emb_ref, tag_ref, hot_ref, embed_ref, grid_ref, sems = rest[5:]
    fetch_embed = pltpu.make_async_copy(embed_hbm, embed_ref, sems.at[0])
    fetch_grid = pltpu.make_async_copy(grid_hbm, grid_ref, sems.at[1])
    fetch_embed.start()
    fetch_grid.start()
    tag_ref[...] = got_ref[:, 32:40, :].astype(F32).reshape(DEVICES * 8, 128)
    tags = tag_ref[pl.ds(0, DEVICES, stride=8), :]
    tags = jnp.transpose(tags)[: 2 * CAP].astype(BF16)
    spread = (iota((DEVICES, SLOTS), 1) // CAP == iota((DEVICES, SLOTS), 0)).astype(F32).astype(BF16)
    wide = jnp.dot(tags, spread, preferred_element_type=F32)
    own = iota((CAP, SLOTS), 1) % CAP == iota((CAP, SLOTS), 0)
    high = jnp.sum(jnp.where(own, wide[:CAP], 0.0), axis=0, keepdims=True)
    low = jnp.sum(jnp.where(own, wide[CAP:], 0.0), axis=0, keepdims=True)
    low_hot = (iota((BLOCK, SLOTS), 0).astype(F32) == low).astype(F32).astype(BF16)
    high_hot = (iota((16, SLOTS), 0).astype(F32) + 1.0 == high).astype(F32).astype(BF16)
    counts = lax.dot_general(low_hot, high_hot, NT, preferred_element_type=F32)
    inverse = 1.0 / jnp.maximum(counts, 1.0)
    high16 = jnp.broadcast_to(high, (16, SLOTS))
    for block in range(BANDS * SECTORS):
        mask = (high16 == block + 1.0).astype(F32).astype(BF16)
        for part in range(BLOCK // 16):
            at = block * BLOCK + part * 16
            hot_ref[at : at + 16, :] = low_hot[part * 16 : part * 16 + 16] * mask
    fetch_embed.wait()
    step = 512
    for at in range(0, SLOTS, step):
        first = at // CAP
        count = step // CAP
        left = got_ref[first : first + count, 0:16, :].reshape(step, 128)
        right = got_ref[first : first + count, 16:32, :].reshape(step, 128)
        raw = jnp.concatenate([left, right], axis=1)
        product = jnp.dot(raw, embed_ref[...], preferred_element_type=F32)
        emb_ref[at : at + step, :] = gelu(product).astype(BF16)
    gain = gain_ref[0:1, :]
    fetch_grid.wait()
    chunk = 512
    for start in range(0, CELLS, chunk):
        total = jnp.dot(hot_ref[start : start + chunk, :], emb_ref[...], preferred_element_type=F32)
        for sub in range(chunk // COLUMN):
            sector = start // COLUMN + sub
            pieces = []
            for band in range(BANDS):
                block = sector * BANDS + band
                row = sub * COLUMN + band * BLOCK
                mean = total[row : row + BLOCK] * inverse[:, block : block + 1]
                static = jnp.concatenate(
                    [
                        grid_ref[band * 8 + r, sector * 8 : sector * 8 + 8, :].astype(F32)
                        for r in range(8)
                    ],
                    axis=0,
                )
                pieces.append(mean + static)
            hidden = jnp.concatenate(pieces, axis=0)
            hidden_ref[sector * COLUMN : (sector + 1) * COLUMN, :] = hidden
            store_normed(sector, norm_rows(hidden, gain), refs)


def combine(got, w_embed, grid_feat, gains):
    return pl.pallas_call(
        combine_kernel,
        out_shape=(pltpu.VMEM((CELLS, D), F32),) + NORMED_SHAPES,
        in_specs=[VMEM, HBM, HBM, VMEM],
        out_specs=(VMEM,) * 6,
        scratch_shapes=[
            pltpu.VMEM((SLOTS, D), BF16),
            pltpu.VMEM((DEVICES * 8, 128), F32),
            pltpu.VMEM((CELLS, SLOTS), BF16),
            pltpu.VMEM((FIN, D), BF16),
            pltpu.VMEM((16, 64, D), BF16),
            pltpu.SemaphoreType.DMA((2,)),
        ],
        compiler_params=PARAMS,
        name="combine",
    )(got, w_embed, grid_feat, gains)


def head_pair(query):
    lane = iota(query.shape, 1) < BLOCK
    zero = jnp.zeros_like(query)
    return jnp.concatenate([jnp.where(lane, query, zero), jnp.where(lane, zero, query)], axis=0)


def fold(values, op):
    rows, width = values.shape
    part = op(values.reshape(rows // BLOCK, BLOCK, width), axis=0)
    part = op(part.reshape(8, 8, width), axis=0)
    return op(part, axis=0, keepdims=True)


def soft(scores):
    highest = fold(scores, jnp.max)
    expo = jnp.exp(scores - highest)
    return expo.astype(BF16), highest, fold(expo, jnp.sum)


LAGS = (0, 2, 3)


def staged(units, stages):
    held = {}
    for turn in range(len(units) + LAGS[-1]):
        for lag, stage in zip(LAGS, stages):
            at = turn - lag
            if 0 <= at < len(units):
                held[at] = stage(units[at], held.get(at))


def near_columns(columns, query_ref, mixed_ref, highest_ref, total_ref):
    units = [(sector, pair) for sector in columns for pair in range(PAIRS)]

    def scored(unit, _):
        sector, pair = unit
        feats = slice(pair * 128, pair * 128 + 128)
        query = head_pair(query_ref[sector * COLUMN : (sector + 1) * COLUMN, feats])
        return lax.dot_general(columns[sector][0](feats), query, NT, preferred_element_type=F32)

    def weighed(unit, scores):
        return soft(scores)

    def summed(unit, held):
        sector, pair = unit
        weights, highest, total = held
        feats = slice(pair * 128, pair * 128 + 128)
        mixed = jnp.dot(columns[sector][1](feats), weights, preferred_element_type=F32)
        at = slice(sector * COLUMN, (sector + 1) * COLUMN)
        for h in range(2):
            head = pair * 2 + h
            lanes = slice(h * COLUMN, (h + 1) * COLUMN)
            mixed_ref[head * BLOCK : (head + 1) * BLOCK, at] = mixed[h * BLOCK : (h + 1) * BLOCK, lanes]
            highest_ref[head : head + 1, at] = highest[:, lanes]
            total_ref[head : head + 1, at] = total[:, lanes]

    staged(units, (scored, weighed, summed))


def inner_column(sector, key_ref, value_ref):
    at = slice((sector - 1) * COLUMN, (sector + 2) * COLUMN)
    return (lambda feats: key_ref[at, feats], lambda feats: value_ref[feats, at])


NEAR_SHAPES = (
    pltpu.VMEM((D, CELLS), F32),
    pltpu.VMEM((HEADS, CELLS), F32),
    pltpu.VMEM((HEADS, CELLS), F32),
)


def project_kernel(
    normed_ref, query_w, key_w, value_w,
    query_ref, key_ref, value_ref, mixed_ref, highest_ref, total_ref,
):
    flat = normed_ref[...]
    query = jnp.dot(flat, query_w[...], preferred_element_type=F32).astype(BF16)
    query_ref[...] = query * BF16(0.125)
    key_ref[...] = jnp.dot(flat, key_w[...], preferred_element_type=F32).astype(BF16)
    value_ref[...] = lax.dot_general(value_w[...], flat, NT, preferred_element_type=F32).astype(BF16)
    columns = {sector: inner_column(sector, key_ref, value_ref) for sector in range(1, SECTORS - 1)}
    near_columns(columns, query_ref, mixed_ref, highest_ref, total_ref)


def project(normed, w_query, w_key, w_value):
    shape = pltpu.VMEM((CELLS, D), BF16)
    return pl.pallas_call(
        project_kernel,
        out_shape=(shape, shape, pltpu.VMEM((D, CELLS), BF16)) + NEAR_SHAPES,
        in_specs=[VMEM] * 4,
        out_specs=(VMEM,) * 6,
        compiler_params=PARAMS,
        cost_estimate=pl.CostEstimate(flops=6 * CELLS * D * D, transcendentals=0, bytes_accessed=5 << 20),
        name="project",
    )(normed, w_query, w_key, w_value)


def sides_of(third_ref, fourth_ref):
    even = lax.axis_index("lon") % 2 == 0
    third = third_ref[...]
    fourth = fourth_ref[...]
    return pick(even, fourth, third), pick(even, third, fourth)


def rows_of(first_ref, second_ref):
    even = lax.axis_index("lat") % 2 == 0
    first = first_ref[...]
    second = second_ref[...]
    return pick(even, second, first), pick(even, first, second)


def corners_kernel(third_ref, fourth_ref, first_ref, second_ref):
    west, east = sides_of(third_ref, fourth_ref)
    even = lax.axis_index("lat") % 2 == 0
    top = jnp.concatenate([west[:BLOCK], east[:BLOCK]], axis=0)
    low = jnp.concatenate([west[BLOCK:], east[BLOCK:]], axis=0)
    first_ref[...] = pick(even, low, top)
    second_ref[...] = pick(even, top, low)


def corners(third, fourth):
    shape = pltpu.VMEM((COLUMN, D), BF16)
    return pl.pallas_call(
        corners_kernel,
        out_shape=(shape, shape),
        in_specs=[VMEM] * 2,
        out_specs=(VMEM,) * 2,
        compiler_params=PARAMS,
        name="corners",
    )(third, fourth)


def near_kernel(
    query_ref, key_ref, value_ref, third_ref, fourth_ref, key_w, value_w, mixed_in, highest_in, total_in,
    mixed_ref, highest_ref, total_ref,
):
    del mixed_in, highest_in, total_in
    outs = (query_ref, mixed_ref, highest_ref, total_ref)
    sides = jnp.concatenate(sides_of(third_ref, fourth_ref), axis=0)
    side_keys = jnp.dot(sides, key_w[...], preferred_element_type=F32).astype(BF16)
    side_values = lax.dot_general(value_w[...], sides, NT, preferred_element_type=F32).astype(BF16)
    columns = {}
    inner = 2 * COLUMN
    columns[0] = (
        lambda feats: jnp.concatenate([side_keys[:COLUMN, feats], key_ref[:inner, feats]], axis=0),
        lambda feats: jnp.concatenate(
            [side_values[feats, :COLUMN], value_ref[feats, :inner]], axis=1
        ),
    )
    columns[SECTORS - 1] = (
        lambda feats: jnp.concatenate(
            [key_ref[CELLS - inner :, feats], side_keys[COLUMN:, feats]], axis=0
        ),
        lambda feats: jnp.concatenate(
            [value_ref[feats, CELLS - inner :], side_values[feats, COLUMN:]], axis=1
        ),
    )
    near_columns(columns, *outs)


def near(query, key, value, third, fourth, w_key, w_value, parts):
    return pl.pallas_call(
        near_kernel,
        out_shape=NEAR_SHAPES,
        in_specs=[VMEM] * 10,
        out_specs=(VMEM,) * 3,
        input_output_aliases={7: 0, 8: 1, 9: 2},
        compiler_params=PARAMS,
        cost_estimate=pl.CostEstimate(flops=8 << 30, transcendentals=4 << 20, bytes_accessed=8 << 20),
        name="near",
    )(query, key, value, third, fourth, w_key, w_value, *parts)


def merge(tiles, head, cells, near_refs, store):
    mixed_ref, highest_ref, total_ref = near_refs
    mixed, highest, total = tiles
    rows = slice(head * BLOCK, (head + 1) * BLOCK)
    highest_near = highest_ref[head : head + 1, cells]
    top = jnp.maximum(highest, highest_near)
    near_part = jnp.exp(highest_near - top)
    far_part = jnp.exp(highest - top)
    weight = total_ref[head : head + 1, cells] * near_part + total * far_part
    near_part = near_part / weight
    far_part = far_part / weight
    store(rows, (mixed_ref[rows, cells] * near_part + mixed * far_part).astype(BF16))


def join(x, y, turn_x):
    if turn_x:
        x = pltpu.roll(x, BLOCK, 1)
    else:
        y = pltpu.roll(y, BLOCK, 1)
    return jnp.where(iota(x.shape, 1) < BLOCK, x, y)


def beyond_grid():
    lat = lax.axis_index("lat")
    return (lat == 0, lat == lax.axis_size("lat") - 1)


def make_far_kernel(last):
    def far_kernel(
        query_ref, mixed_ref, highest_ref, total_ref, first_ref, second_ref,
        hidden_ref, gain_ref, key_w, value_w, out_w, *rest,
    ):
        new_ref, key_f, value_f = rest[:3]
        refs = rest[3:-1]
        att_ref = rest[-1]
        near_refs = (mixed_ref, highest_ref, total_ref)
        for band, rows in enumerate(rows_of(first_ref, second_ref)):
            key_f[band] = jnp.dot(rows, key_w[...], preferred_element_type=F32).astype(BF16)
            value_f[band] = lax.dot_general(
                value_w[...], rows, NT, preferred_element_type=F32
            ).astype(BF16)
        beyond = beyond_grid()
        span = 4 * BLOCK

        def hide(scores):
            second = iota((BLOCK, 2 * COLUMN), 1) % COLUMN >= BLOCK
            return jnp.concatenate(
                [
                    jnp.where(second, NEG, scores[:BLOCK]),
                    scores[BLOCK : 3 * BLOCK],
                    jnp.where(second, scores[3 * BLOCK :], NEG),
                ],
                axis=0,
            )

        def scored(unit, _):
            step, pair, band = unit
            feats = slice(pair * 128, pair * 128 + 128)
            first = (step * 2 + 1) * COLUMN + band * BLOCK
            query = jnp.concatenate(
                [
                    query_ref[first : first + BLOCK, feats],
                    query_ref[first + COLUMN : first + COLUMN + BLOCK, feats],
                ],
                axis=0,
            )
            keys = key_f[band, step * COLUMN : step * COLUMN + span, feats]
            return hide(lax.dot_general(keys, head_pair(query), NT, preferred_element_type=F32))

        def weighed(unit, scores):
            return soft(scores)

        def summed(unit, held):
            step, pair, band = unit
            weights, highest, total = held
            feats = slice(pair * 128, pair * 128 + 128)
            values = value_f[band, feats, step * COLUMN : step * COLUMN + span]
            mixed = jnp.dot(values, weights, preferred_element_type=F32)
            waiting[unit] = (mixed, jnp.where(beyond[band], NEG, highest), total)
            if band == 0:
                return
            upper = waiting.pop((step, pair, 0))
            lower = waiting.pop(unit)
            for h in range(2):
                lanes = slice(h * COLUMN, (h + 1) * COLUMN)
                here = (slice(h * BLOCK, (h + 1) * BLOCK), slice(None), slice(None))
                for second in range(2):
                    tiles = [
                        join(x[part, lanes], y[part, lanes], second == 1)
                        for x, y, part in zip(upper, lower, here)
                    ]
                    at = (step * 2 + 1 + second) * COLUMN
                    cells = slice(at, at + COLUMN)

                    def store(rows, value):
                        att_ref[rows, cells] = value

                    merge(tiles, pair * 2 + h, cells, near_refs, store)

        waiting = {}
        staged(
            [
                (step, pair, band)
                for step in range(SECTORS // 2 - 1)
                for pair in range(PAIRS)
                for band in range(BANDS)
            ],
            (scored, weighed, summed),
        )
        gain = gain_ref[...]
        for at in range(COLUMN, CELLS - COLUMN, 256):
            update = lax.dot_general(
                att_ref[:, at : at + 256], out_w[...], TN, preferred_element_type=F32
            )
            hidden = hidden_ref[at : at + 256, :] + update
            new_ref[at : at + 256, :] = hidden
            if not last:
                normed = norm_rows(hidden, gain)
                for sub in range(256 // COLUMN):
                    store_normed(
                        at // COLUMN + sub,
                        normed[sub * COLUMN : (sub + 1) * COLUMN],
                        refs + (None, None),
                    )

    return far_kernel


def far(query, parts, first, second, hidden, gain, w_key, w_value, w_out, last):
    out_shape = (
        pltpu.VMEM((CELLS, D), F32),
        pltpu.VMEM((BANDS, HALO, D), BF16),
        pltpu.VMEM((BANDS, D, HALO), BF16),
    )
    if not last:
        out_shape = out_shape + NORMED_SHAPES[:3]
    return pl.pallas_call(
        make_far_kernel(last),
        out_shape=out_shape,
        in_specs=[VMEM] * 11,
        out_specs=(VMEM,) * len(out_shape),
        scratch_shapes=[pltpu.VMEM((D, CELLS), BF16)],
        compiler_params=PARAMS,
        cost_estimate=pl.CostEstimate(flops=8 << 30, transcendentals=4 << 20, bytes_accessed=8 << 20),
        name="far",
    )(query, *parts, first, second, hidden, gain, w_key, w_value, w_out)


def make_edge_kernel(last):
    def edge_kernel(
        query_ref, mixed_ref, highest_ref, total_ref, first_ref, second_ref,
        hidden_ref, gain_ref, key_w, value_w, out_w, key_f, value_f, *rest,
    ):
        near_refs = (mixed_ref, highest_ref, total_ref)
        att_ref = rest[-1]
        if last:
            inner_ref, out_ref, edge_ref = rest[:3]
        else:
            new_ref = rest[4]
            refs = rest[5:10]
        rows = jnp.concatenate(rows_of(first_ref, second_ref), axis=0)
        corner_keys = jnp.dot(rows, key_w[...], preferred_element_type=F32).astype(BF16)
        corner_values = lax.dot_general(
            value_w[...], rows, NT, preferred_element_type=F32
        ).astype(BF16)
        beyond = beyond_grid()
        starts = (0, HALO - 2 * BLOCK)

        def scored(unit, _):
            side, pair, band = unit
            feats = slice(pair * 128, pair * 128 + 128)
            first = side * (SECTORS - 1) * COLUMN + band * BLOCK
            corner = (band * 2 + side) * BLOCK
            keys = jnp.concatenate(
                [
                    key_f[band, starts[side] : starts[side] + 2 * BLOCK, feats],
                    corner_keys[corner : corner + BLOCK, feats],
                ],
                axis=0,
            )
            query = head_pair(query_ref[first : first + BLOCK, feats])
            return lax.dot_general(keys, query, NT, preferred_element_type=F32)

        def weighed(unit, scores):
            return soft(scores)

        def summed(unit, held):
            side, pair, band = unit
            weights, highest, total = held
            feats = slice(pair * 128, pair * 128 + 128)
            corner = (band * 2 + side) * BLOCK
            values = jnp.concatenate(
                [
                    value_f[band, feats, starts[side] : starts[side] + 2 * BLOCK],
                    corner_values[feats, corner : corner + BLOCK],
                ],
                axis=1,
            )
            mixed = jnp.dot(values, weights, preferred_element_type=F32)
            waiting[unit] = (mixed, jnp.where(beyond[band], NEG, highest), total)
            if band == 0:
                return
            upper = waiting.pop((side, pair, 0))
            lower = waiting.pop(unit)
            for h in range(2):
                here = (slice(h * BLOCK, (h + 1) * BLOCK), slice(None), slice(None))
                tiles = [join(x[part], y[part], h == 1) for x, y, part in zip(upper, lower, here)]
                at = side * (SECTORS - 1) * COLUMN
                lanes = slice(side * COLUMN, (side + 1) * COLUMN)

                def store(rows, value):
                    att_ref[rows, lanes] = value

                merge(tiles, pair * 2 + h, slice(at, at + COLUMN), near_refs, store)

        waiting = {}
        staged(
            [
                (side, pair, band)
                for side in range(2)
                for pair in range(PAIRS)
                for band in range(BANDS)
            ],
            (scored, weighed, summed),
        )
        update = lax.dot_general(att_ref[...], out_w[...], TN, preferred_element_type=F32)
        gain = gain_ref[...]
        for side in range(2):
            at = side * (CELLS - COLUMN)
            hidden = hidden_ref[at : at + COLUMN, :] + update[side * COLUMN : (side + 1) * COLUMN]
            if last:
                edge_ref[side * COLUMN : (side + 1) * COLUMN, :] = hidden
                continue
            new_ref[at : at + COLUMN, :] = hidden
            normed = norm_rows(hidden, gain)
            store_normed(at // COLUMN, normed, refs)
        if last:
            for band in range(BANDS):
                for r in range(8):
                    pieces = []
                    for sector in range(SECTORS):
                        at = (sector * BANDS + band) * BLOCK + r * 8
                        if sector == 0:
                            pieces.append(edge_ref[at : at + 8, :])
                        elif sector == SECTORS - 1:
                            at = at - CELLS + 2 * COLUMN
                            pieces.append(edge_ref[at : at + 8, :])
                        else:
                            pieces.append(inner_ref[at : at + 8, :])
                    out_ref[band * 8 + r] = jnp.concatenate(pieces, axis=0).astype(BF16)

    return edge_kernel


def edges(query, parts, first, second, hidden, gain, w_key, w_value, w_out, inner, last):
    new, key_f, value_f, *normed = inner
    scratch = [pltpu.VMEM((D, 2 * COLUMN), BF16)]
    if last:
        scratch = [pltpu.VMEM((2 * COLUMN, D), F32)] + scratch
        out_shape = jax.ShapeDtypeStruct((16, 64, D), BF16)
        out_specs = VMEM
        aliases = {}
    else:
        out_shape = (pltpu.VMEM((CELLS, D), F32),) + NORMED_SHAPES
        out_specs = (VMEM,) * 6
        aliases = {13: 0, 14: 1, 15: 2, 16: 3}
    return pl.pallas_call(
        make_edge_kernel(last),
        out_shape=out_shape,
        in_specs=[VMEM] * (14 + len(normed)),
        out_specs=out_specs,
        scratch_shapes=scratch,
        input_output_aliases=aliases,
        compiler_params=PARAMS,
        name="edges",
    )(query, *parts, first, second, hidden, gain, w_key, w_value, w_out, key_f, value_f, new, *normed)


def local(
    obs_feat, obs_owner, obs_cell, obs_valid, grid_feat,
    w_embed, gains, w_query, w_key, w_value, w_out,
):
    send = dispatch(
        off_chip(obs_owner.reshape(1, OBS)),
        off_chip(obs_cell.reshape(1, OBS)),
        off_chip(obs_valid.reshape(1, OBS)),
        off_chip(obs_feat),
    )
    got = lax.all_to_all(on_chip(send), ("lat", "lon"), split_axis=0, concat_axis=0, tiled=True)
    lat_count = lax.axis_size("lat")
    lon_count = lax.axis_size("lon")
    hidden, *normed = combine(got, off_chip(w_embed), off_chip(grid_feat), gains)
    lat_first = [(i, i ^ 1) for i in range(lat_count)]
    lat_second = [(0, 0), (lat_count - 1, lat_count - 1)]
    for i in range(1, lat_count - 1, 2):
        lat_second += [(i, i + 1), (i + 1, i)]
    lat_round = [(i, (((i + 1) ^ 1) - 1) % lat_count) for i in range(lat_count)]
    lon_first = [(i, i ^ 1) for i in range(lon_count)]
    lon_second = [(i, (((i + 1) ^ 1) - 1) % lon_count) for i in range(lon_count)]
    for layer in range(LAYERS):
        last = layer == LAYERS - 1
        key_w = on_chip(w_key[layer])
        value_w = on_chip(jnp.transpose(w_value[layer]))
        hidden = on_chip(hidden)
        flat, *trades = [on_chip(item) for item in normed]
        third = lax.ppermute(trades[2], "lon", lon_first)
        fourth = lax.ppermute(trades[3], "lon", lon_second)
        second = lax.ppermute(trades[1], "lat", lat_second)
        first = lax.ppermute(trades[0], "lat", lat_first)
        query, key, value, *parts = project(flat, on_chip(w_query[layer]), key_w, value_w)
        query = on_chip(query)
        corner = corners(third, fourth)
        corner_second = lax.ppermute(on_chip(corner[1]), "lat", lat_round)
        corner_first = lax.ppermute(on_chip(corner[0]), "lat", lat_first)
        parts = [on_chip(part) for part in parts]
        parts = near(
            query, on_chip(key), on_chip(value), third, fourth, key_w, value_w, parts
        )
        parts = [on_chip(part) for part in parts]
        following = min(layer + 1, LAYERS - 1)
        gain = gains[following : following + 1]
        out_w = on_chip(w_out[layer])
        inner = far(query, parts, first, second, hidden, gain, key_w, value_w, out_w, last)
        inner = [on_chip(item) for item in inner]
        result = edges(
            query, parts, corner_first, corner_second, hidden, gain, key_w, value_w, out_w, inner, last
        )
        if not last:
            hidden, *normed = result
    return result


def solution(mesh):
    placed = (
        P(("lat", "lon"), None),
        P(("lat", "lon"), None),
        P(("lat", "lon")),
        P(("lat", "lon")),
        P("lat", "lon", None),
        P(), P(), P(), P(), P(), P(),
    )
    return jax.shard_map(
        local, mesh=mesh, in_specs=placed, out_specs=P("lat", "lon", None), check_vma=False
    )
```

```python
import jax
import jax.numpy as jnp
from jax import lax
from jax.experimental import pallas as pl
from jax.experimental.pallas import tpu as pltpu
from jax.sharding import PartitionSpec as P

HEADS = 8
LAYERS = 2
D = 512
FIN = 256
DEVICES = 128
CAP = 16
ROWS = 40
OBS = 1024
CELLS = 1024
SLOTS = DEVICES * CAP
BLOCK = 64
BANDS = 2
SECTORS = 8
FRAME = SECTORS + 2
PAIRS = HEADS // 2
COLUMN = BANDS * BLOCK
NEG = -1e30
F32 = jnp.float32
BF16 = jnp.bfloat16

VMEM = pl.BlockSpec(memory_space=pltpu.VMEM)
HBM = pl.BlockSpec(memory_space=pl.ANY)
PARAMS = pltpu.CompilerParams(vmem_limit_bytes=40 * 1024 * 1024)
WIDE = FRAME * BLOCK
HALO = SECTORS * BLOCK
NT = (((1,), (1,)), ((), ()))
TN = (((0,), (0,)), ((), ()))


def iota(shape, axis):
    return lax.broadcasted_iota(jnp.int32, shape, axis)


def dispatch_kernel(
    owner_hbm, cell_hbm, valid_hbm, feat_hbm, send_ref, owner_ref, cell_ref, valid_ref, feat_ref, sems
):
    pairs = ((owner_hbm, owner_ref), (cell_hbm, cell_ref), (valid_hbm, valid_ref), (feat_hbm, feat_ref))
    copies = [pltpu.make_async_copy(a, b, sems.at[i]) for i, (a, b) in enumerate(pairs)]
    for copy in copies:
        copy.start()
    for copy in copies[:3]:
        copy.wait()
    owner = owner_ref[...]
    cell = cell_ref[...]
    valid = valid_ref[...]
    wide = 256
    earlier = (iota((wide, wide), 0) < iota((wide, wide), 1)).astype(F32).astype(BF16)
    carry = jnp.zeros((DEVICES, 1), F32)
    ranks = []
    chosen = []
    for at in range(0, OBS, wide):
        hot = (iota((DEVICES, wide), 0) == owner[:, at : at + wide]).astype(F32)
        before = jnp.dot(hot.astype(BF16), earlier, preferred_element_type=F32) + carry
        ranks.append(jnp.sum(hot * before, axis=0, keepdims=True))
        carry = carry + jnp.sum(hot, axis=1, keepdims=True)
        chosen.append(hot.astype(BF16))
    rank = jnp.concatenate(ranks, axis=1).astype(jnp.int32)
    hot_all = jnp.concatenate(chosen, axis=1)
    row = cell // 64
    col = cell % 64
    high = (col // 8) * BANDS + row // 8 + 1
    low = (row % 8) * 8 + col % 8
    usable = valid == 1
    high = jnp.where(usable, high, 0)
    low = jnp.where(usable, low, 0)
    lane = iota((128, OBS), 0)
    part = jnp.where(lane < CAP, high, jnp.where(lane < 2 * CAP, low, 0))
    entry = jnp.where(lane % CAP == rank, part, 0).astype(F32).astype(BF16)
    tags = lax.dot_general(hot_all, entry, NT, preferred_element_type=F32)
    send_ref[:, 32:40, :] = jnp.broadcast_to(tags[:, None, :], (DEVICES, 8, 128)).astype(BF16)
    target = owner * CAP + rank
    copies[3].wait()
    feat = feat_ref[...]
    step = 256
    for at in range(0, SLOTS, step):
        pick = (iota((step, OBS), 0) + at == target).astype(F32).astype(BF16)
        rows = jnp.dot(pick, feat, preferred_element_type=F32).astype(BF16)
        first = at // CAP
        count = step // CAP
        send_ref[first : first + count, 0:16, :] = rows[:, :128].reshape(count, CAP, 128)
        send_ref[first : first + count, 16:32, :] = rows[:, 128:].reshape(count, CAP, 128)


def dispatch(owner, cell, valid, feat):
    return pl.pallas_call(
        dispatch_kernel,
        out_shape=pltpu.VMEM((DEVICES, ROWS, 128), BF16),
        in_specs=[HBM] * 4,
        out_specs=VMEM,
        scratch_shapes=[pltpu.VMEM((1, OBS), jnp.int32)] * 3
        + [pltpu.VMEM((OBS, FIN), BF16), pltpu.SemaphoreType.DMA((4,))],
        compiler_params=PARAMS,
        name="dispatch",
    )(owner, cell, valid, feat)


def on_chip(array):
    return pltpu.with_memory_space_constraint(array, pltpu.VMEM)


def off_chip(array):
    return pltpu.with_memory_space_constraint(array, pltpu.HBM)


def norm_rows(hidden, gain):
    scale = lax.rsqrt(jnp.mean(hidden * hidden, axis=-1, keepdims=True) + 1e-06)
    return (hidden * scale * gain).astype(BF16)


def pick(choose, x, y):
    return jnp.where(choose, x, y)


def store_normed(sector, rows, refs):
    normed_ref, first_ref, second_ref, third_ref, fourth_ref = refs
    here = slice(sector * BLOCK, (sector + 1) * BLOCK)
    normed_ref[sector * COLUMN : (sector + 1) * COLUMN, :] = rows
    even = lax.axis_index("lat") % 2 == 0
    top = rows[:BLOCK]
    low = rows[BLOCK:]
    first_ref[here, :] = pick(even, low, top)
    second_ref[here, :] = pick(even, top, low)
    if sector == 0:
        third_ref[...] = rows
        fourth_ref[...] = rows
    if sector == SECTORS - 1:
        even = lax.axis_index("lon") % 2 == 0
        third_ref[...] = pick(even, rows, third_ref[...])
        fourth_ref[...] = pick(even, fourth_ref[...], rows)


NORMED_SHAPES = (
    pltpu.VMEM((CELLS, D), BF16),
    pltpu.VMEM((HALO, D), BF16),
    pltpu.VMEM((HALO, D), BF16),
    pltpu.VMEM((COLUMN, D), BF16),
    pltpu.VMEM((COLUMN, D), BF16),
)


def gelu(x):
    inner = x * (0.7978845608028654 + (0.7978845608028654 * 0.044715) * (x * x))
    half = 0.5 * x
    return half + half * jnp.tanh(inner)


def combine_kernel(
    got_ref, embed_hbm, grid_hbm, gain_ref, hidden_ref, *rest
):
    refs = rest[:5]
    emb_ref, tag_ref, hot_ref, embed_ref, grid_ref, sems = rest[5:]
    fetch_embed = pltpu.make_async_copy(embed_hbm, embed_ref, sems.at[0])
    fetch_grid = pltpu.make_async_copy(grid_hbm, grid_ref, sems.at[1])
    fetch_embed.start()
    fetch_grid.start()
    tag_ref[...] = got_ref[:, 32:40, :].astype(F32).reshape(DEVICES * 8, 128)
    tags = tag_ref[pl.ds(0, DEVICES, stride=8), :]
    tags = jnp.transpose(tags)[: 2 * CAP].astype(BF16)
    spread = (iota((DEVICES, SLOTS), 1) // CAP == iota((DEVICES, SLOTS), 0)).astype(F32).astype(BF16)
    wide = jnp.dot(tags, spread, preferred_element_type=F32)
    own = iota((CAP, SLOTS), 1) % CAP == iota((CAP, SLOTS), 0)
    high = jnp.sum(jnp.where(own, wide[:CAP], 0.0), axis=0, keepdims=True)
    low = jnp.sum(jnp.where(own, wide[CAP:], 0.0), axis=0, keepdims=True)
    low_hot = (iota((BLOCK, SLOTS), 0).astype(F32) == low).astype(F32).astype(BF16)
    high_hot = (iota((16, SLOTS), 0).astype(F32) + 1.0 == high).astype(F32).astype(BF16)
    counts = lax.dot_general(low_hot, high_hot, NT, preferred_element_type=F32)
    inverse = 1.0 / jnp.maximum(counts, 1.0)
    high16 = jnp.broadcast_to(high, (16, SLOTS))
    for block in range(BANDS * SECTORS):
        mask = (high16 == block + 1.0).astype(F32).astype(BF16)
        for part in range(BLOCK // 16):
            at = block * BLOCK + part * 16
            hot_ref[at : at + 16, :] = low_hot[part * 16 : part * 16 + 16] * mask
    fetch_embed.wait()
    step = 512
    for at in range(0, SLOTS, step):
        first = at // CAP
        count = step // CAP
        left = got_ref[first : first + count, 0:16, :].reshape(step, 128)
        right = got_ref[first : first + count, 16:32, :].reshape(step, 128)
        raw = jnp.concatenate([left, right], axis=1)
        product = jnp.dot(raw, embed_ref[...], preferred_element_type=F32)
        emb_ref[at : at + step, :] = gelu(product).astype(BF16)
    gain = gain_ref[0:1, :]
    fetch_grid.wait()
    chunk = 512
    for start in range(0, CELLS, chunk):
        total = jnp.dot(hot_ref[start : start + chunk, :], emb_ref[...], preferred_element_type=F32)
        for sub in range(chunk // COLUMN):
            sector = start // COLUMN + sub
            pieces = []
            for band in range(BANDS):
                block = sector * BANDS + band
                row = sub * COLUMN + band * BLOCK
                mean = total[row : row + BLOCK] * inverse[:, block : block + 1]
                static = jnp.concatenate(
                    [
                        grid_ref[band * 8 + r, sector * 8 : sector * 8 + 8, :].astype(F32)
                        for r in range(8)
                    ],
                    axis=0,
                )
                pieces.append(mean + static)
            hidden = jnp.concatenate(pieces, axis=0)
            hidden_ref[sector * COLUMN : (sector + 1) * COLUMN, :] = hidden
            store_normed(sector, norm_rows(hidden, gain), refs)


def combine(got, w_embed, grid_feat, gains):
    return pl.pallas_call(
        combine_kernel,
        out_shape=(pltpu.VMEM((CELLS, D), F32),) + NORMED_SHAPES,
        in_specs=[VMEM, HBM, HBM, VMEM],
        out_specs=(VMEM,) * 6,
        scratch_shapes=[
            pltpu.VMEM((SLOTS, D), BF16),
            pltpu.VMEM((DEVICES * 8, 128), F32),
            pltpu.VMEM((CELLS, SLOTS), BF16),
            pltpu.VMEM((FIN, D), BF16),
            pltpu.VMEM((16, 64, D), BF16),
            pltpu.SemaphoreType.DMA((2,)),
        ],
        compiler_params=PARAMS,
        name="combine",
    )(got, w_embed, grid_feat, gains)


def head_pair(query):
    lane = iota(query.shape, 1) < BLOCK
    zero = jnp.zeros_like(query)
    return jnp.concatenate([jnp.where(lane, query, zero), jnp.where(lane, zero, query)], axis=0)


def fold(values, op):
    rows, width = values.shape
    part = op(values.reshape(rows // BLOCK, BLOCK, width), axis=0)
    part = op(part.reshape(8, 8, width), axis=0)
    return op(part, axis=0, keepdims=True)


def soft(scores):
    highest = fold(scores, jnp.max)
    expo = jnp.exp(scores - highest)
    return expo.astype(BF16), highest, fold(expo, jnp.sum)


LAGS = (0, 3, 4)


def staged(units, stages):
    held = {}
    for turn in range(len(units) + LAGS[-1]):
        for lag, stage in zip(LAGS, stages):
            at = turn - lag
            if 0 <= at < len(units):
                held[at] = stage(units[at], held.get(at))


def near_columns(columns, query_ref, mixed_ref, highest_ref, total_ref):
    units = [(sector, pair) for sector in columns for pair in range(PAIRS)]

    def scored(unit, _):
        sector, pair = unit
        feats = slice(pair * 128, pair * 128 + 128)
        query = head_pair(query_ref[sector * COLUMN : (sector + 1) * COLUMN, feats])
        return lax.dot_general(columns[sector][0](feats), query, NT, preferred_element_type=F32)

    def weighed(unit, scores):
        return soft(scores)

    def summed(unit, held):
        sector, pair = unit
        weights, highest, total = held
        feats = slice(pair * 128, pair * 128 + 128)
        mixed = jnp.dot(columns[sector][1](feats), weights, preferred_element_type=F32)
        at = slice(sector * COLUMN, (sector + 1) * COLUMN)
        for h in range(2):
            head = pair * 2 + h
            lanes = slice(h * COLUMN, (h + 1) * COLUMN)
            mixed_ref[head * BLOCK : (head + 1) * BLOCK, at] = mixed[h * BLOCK : (h + 1) * BLOCK, lanes]
            highest_ref[head : head + 1, at] = highest[:, lanes]
            total_ref[head : head + 1, at] = total[:, lanes]

    staged(units, (scored, weighed, summed))


def inner_column(sector, key_ref, value_ref):
    at = slice((sector - 1) * COLUMN, (sector + 2) * COLUMN)
    return (lambda feats: key_ref[at, feats], lambda feats: value_ref[feats, at])


NEAR_SHAPES = (
    pltpu.VMEM((D, CELLS), F32),
    pltpu.VMEM((HEADS, CELLS), F32),
    pltpu.VMEM((HEADS, CELLS), F32),
)


def project_kernel(
    normed_ref, query_w, key_w, value_w,
    query_ref, key_ref, value_ref, mixed_ref, highest_ref, total_ref,
):
    flat = normed_ref[...]
    query = jnp.dot(flat, query_w[...], preferred_element_type=F32).astype(BF16)
    query_ref[...] = query * BF16(0.125)
    key_ref[...] = jnp.dot(flat, key_w[...], preferred_element_type=F32).astype(BF16)
    value_ref[...] = lax.dot_general(value_w[...], flat, NT, preferred_element_type=F32).astype(BF16)
    columns = {sector: inner_column(sector, key_ref, value_ref) for sector in range(1, SECTORS - 1)}
    near_columns(columns, query_ref, mixed_ref, highest_ref, total_ref)


def project(normed, w_query, w_key, w_value):
    shape = pltpu.VMEM((CELLS, D), BF16)
    return pl.pallas_call(
        project_kernel,
        out_shape=(shape, shape, pltpu.VMEM((D, CELLS), BF16)) + NEAR_SHAPES,
        in_specs=[VMEM] * 4,
        out_specs=(VMEM,) * 6,
        compiler_params=PARAMS,
        cost_estimate=pl.CostEstimate(flops=6 * CELLS * D * D, transcendentals=0, bytes_accessed=5 << 20),
        name="project",
    )(normed, w_query, w_key, w_value)


def sides_of(third_ref, fourth_ref):
    even = lax.axis_index("lon") % 2 == 0
    third = third_ref[...]
    fourth = fourth_ref[...]
    return pick(even, fourth, third), pick(even, third, fourth)


def rows_of(first_ref, second_ref):
    even = lax.axis_index("lat") % 2 == 0
    first = first_ref[...]
    second = second_ref[...]
    return pick(even, second, first), pick(even, first, second)


def corners_kernel(third_ref, fourth_ref, first_ref, second_ref):
    west, east = sides_of(third_ref, fourth_ref)
    even = lax.axis_index("lat") % 2 == 0
    top = jnp.concatenate([west[:BLOCK], east[:BLOCK]], axis=0)
    low = jnp.concatenate([west[BLOCK:], east[BLOCK:]], axis=0)
    first_ref[...] = pick(even, low, top)
    second_ref[...] = pick(even, top, low)


def corners(third, fourth):
    shape = pltpu.VMEM((COLUMN, D), BF16)
    return pl.pallas_call(
        corners_kernel,
        out_shape=(shape, shape),
        in_specs=[VMEM] * 2,
        out_specs=(VMEM,) * 2,
        compiler_params=PARAMS,
        name="corners",
    )(third, fourth)


def near_kernel(
    query_ref, key_ref, value_ref, third_ref, fourth_ref, key_w, value_w, mixed_in, highest_in, total_in,
    mixed_ref, highest_ref, total_ref,
):
    del mixed_in, highest_in, total_in
    outs = (query_ref, mixed_ref, highest_ref, total_ref)
    sides = jnp.concatenate(sides_of(third_ref, fourth_ref), axis=0)
    side_keys = jnp.dot(sides, key_w[...], preferred_element_type=F32).astype(BF16)
    side_values = lax.dot_general(value_w[...], sides, NT, preferred_element_type=F32).astype(BF16)
    columns = {}
    inner = 2 * COLUMN
    columns[0] = (
        lambda feats: jnp.concatenate([side_keys[:COLUMN, feats], key_ref[:inner, feats]], axis=0),
        lambda feats: jnp.concatenate(
            [side_values[feats, :COLUMN], value_ref[feats, :inner]], axis=1
        ),
    )
    columns[SECTORS - 1] = (
        lambda feats: jnp.concatenate(
            [key_ref[CELLS - inner :, feats], side_keys[COLUMN:, feats]], axis=0
        ),
        lambda feats: jnp.concatenate(
            [value_ref[feats, CELLS - inner :], side_values[feats, COLUMN:]], axis=1
        ),
    )
    near_columns(columns, *outs)


def near(query, key, value, third, fourth, w_key, w_value, parts):
    return pl.pallas_call(
        near_kernel,
        out_shape=NEAR_SHAPES,
        in_specs=[VMEM] * 10,
        out_specs=(VMEM,) * 3,
        input_output_aliases={7: 0, 8: 1, 9: 2},
        compiler_params=PARAMS,
        cost_estimate=pl.CostEstimate(flops=8 << 30, transcendentals=4 << 20, bytes_accessed=8 << 20),
        name="near",
    )(query, key, value, third, fourth, w_key, w_value, *parts)


def merge(tiles, head, cells, near_refs, store):
    mixed_ref, highest_ref, total_ref = near_refs
    mixed, highest, total = tiles
    rows = slice(head * BLOCK, (head + 1) * BLOCK)
    highest_near = highest_ref[head : head + 1, cells]
    top = jnp.maximum(highest, highest_near)
    near_part = jnp.exp(highest_near - top)
    far_part = jnp.exp(highest - top)
    weight = total_ref[head : head + 1, cells] * near_part + total * far_part
    near_part = near_part / weight
    far_part = far_part / weight
    store(rows, (mixed_ref[rows, cells] * near_part + mixed * far_part).astype(BF16))


def join(x, y, turn_x):
    if turn_x:
        x = pltpu.roll(x, BLOCK, 1)
    else:
        y = pltpu.roll(y, BLOCK, 1)
    return jnp.where(iota(x.shape, 1) < BLOCK, x, y)


def beyond_grid():
    lat = lax.axis_index("lat")
    return (lat == 0, lat == lax.axis_size("lat") - 1)


def make_far_kernel(last):
    def far_kernel(
        query_ref, mixed_ref, highest_ref, total_ref, first_ref, second_ref,
        hidden_ref, gain_ref, key_w, value_w, out_w, *rest,
    ):
        new_ref, key_f, value_f = rest[:3]
        refs = rest[3:-1]
        att_ref = rest[-1]
        near_refs = (mixed_ref, highest_ref, total_ref)
        for band, rows in enumerate(rows_of(first_ref, second_ref)):
            key_f[band] = jnp.dot(rows, key_w[...], preferred_element_type=F32).astype(BF16)
            value_f[band] = lax.dot_general(
                value_w[...], rows, NT, preferred_element_type=F32
            ).astype(BF16)
        beyond = beyond_grid()
        span = 4 * BLOCK

        def hide(scores):
            second = iota((BLOCK, 2 * COLUMN), 1) % COLUMN >= BLOCK
            return jnp.concatenate(
                [
                    jnp.where(second, NEG, scores[:BLOCK]),
                    scores[BLOCK : 3 * BLOCK],
                    jnp.where(second, scores[3 * BLOCK :], NEG),
                ],
                axis=0,
            )

        def scored(unit, _):
            step, pair, band = unit
            feats = slice(pair * 128, pair * 128 + 128)
            first = (step * 2 + 1) * COLUMN + band * BLOCK
            query = jnp.concatenate(
                [
                    query_ref[first : first + BLOCK, feats],
                    query_ref[first + COLUMN : first + COLUMN + BLOCK, feats],
                ],
                axis=0,
            )
            keys = key_f[band, step * COLUMN : step * COLUMN + span, feats]
            return hide(lax.dot_general(keys, head_pair(query), NT, preferred_element_type=F32))

        def weighed(unit, scores):
            return soft(scores)

        def summed(unit, held):
            step, pair, band = unit
            weights, highest, total = held
            feats = slice(pair * 128, pair * 128 + 128)
            values = value_f[band, feats, step * COLUMN : step * COLUMN + span]
            mixed = jnp.dot(values, weights, preferred_element_type=F32)
            waiting[unit] = (mixed, jnp.where(beyond[band], NEG, highest), total)
            if band == 0:
                return
            upper = waiting.pop((step, pair, 0))
            lower = waiting.pop(unit)
            for h in range(2):
                lanes = slice(h * COLUMN, (h + 1) * COLUMN)
                here = (slice(h * BLOCK, (h + 1) * BLOCK), slice(None), slice(None))
                for second in range(2):
                    tiles = [
                        join(x[part, lanes], y[part, lanes], second == 1)
                        for x, y, part in zip(upper, lower, here)
                    ]
                    at = (step * 2 + 1 + second) * COLUMN
                    cells = slice(at, at + COLUMN)

                    def store(rows, value):
                        att_ref[rows, cells] = value

                    merge(tiles, pair * 2 + h, cells, near_refs, store)

        waiting = {}
        staged(
            [
                (step, pair, band)
                for step in range(SECTORS // 2 - 1)
                for pair in range(PAIRS)
                for band in range(BANDS)
            ],
            (scored, weighed, summed),
        )
        gain = gain_ref[...]
        for at in range(COLUMN, CELLS - COLUMN, 256):
            update = lax.dot_general(
                att_ref[:, at : at + 256], out_w[...], TN, preferred_element_type=F32
            )
            hidden = hidden_ref[at : at + 256, :] + update
            new_ref[at : at + 256, :] = hidden
            if not last:
                normed = norm_rows(hidden, gain)
                for sub in range(256 // COLUMN):
                    store_normed(
                        at // COLUMN + sub,
                        normed[sub * COLUMN : (sub + 1) * COLUMN],
                        refs + (None, None),
                    )

    return far_kernel


def far(query, parts, first, second, hidden, gain, w_key, w_value, w_out, last):
    out_shape = (
        pltpu.VMEM((CELLS, D), F32),
        pltpu.VMEM((BANDS, HALO, D), BF16),
        pltpu.VMEM((BANDS, D, HALO), BF16),
    )
    if not last:
        out_shape = out_shape + NORMED_SHAPES[:3]
    return pl.pallas_call(
        make_far_kernel(last),
        out_shape=out_shape,
        in_specs=[VMEM] * 11,
        out_specs=(VMEM,) * len(out_shape),
        scratch_shapes=[pltpu.VMEM((D, CELLS), BF16)],
        compiler_params=PARAMS,
        cost_estimate=pl.CostEstimate(flops=8 << 30, transcendentals=4 << 20, bytes_accessed=8 << 20),
        name="far",
    )(query, *parts, first, second, hidden, gain, w_key, w_value, w_out)


def make_edge_kernel(last):
    def edge_kernel(
        query_ref, mixed_ref, highest_ref, total_ref, first_ref, second_ref,
        hidden_ref, gain_ref, key_w, value_w, out_w, key_f, value_f, *rest,
    ):
        near_refs = (mixed_ref, highest_ref, total_ref)
        att_ref = rest[-1]
        if last:
            inner_ref, out_ref, edge_ref, stage_ref, side_ref, sems = rest[:6]
            for band in range(BANDS):
                for r in range(8):
                    pieces = []
                    for sector in range(1, SECTORS - 1):
                        at = (sector * BANDS + band) * BLOCK + r * 8
                        pieces.append(inner_ref[at : at + 8, :])
                    stage_ref[band * 8 + r] = jnp.concatenate(pieces, axis=0).astype(BF16)
            copies = [
                pltpu.make_async_copy(stage_ref, out_ref.at[:, pl.ds(8, 48), :], sems.at[0]),
                pltpu.make_async_copy(side_ref.at[0], out_ref.at[:, pl.ds(0, 8), :], sems.at[1]),
                pltpu.make_async_copy(side_ref.at[1], out_ref.at[:, pl.ds(56, 8), :], sems.at[2]),
            ]
            copies[0].start()
        else:
            new_ref = rest[4]
            refs = rest[5:10]
        rows = jnp.concatenate(rows_of(first_ref, second_ref), axis=0)
        corner_keys = jnp.dot(rows, key_w[...], preferred_element_type=F32).astype(BF16)
        corner_values = lax.dot_general(
            value_w[...], rows, NT, preferred_element_type=F32
        ).astype(BF16)
        beyond = beyond_grid()
        starts = (0, HALO - 2 * BLOCK)

        def scored(unit, _):
            side, pair, band = unit
            feats = slice(pair * 128, pair * 128 + 128)
            first = side * (SECTORS - 1) * COLUMN + band * BLOCK
            corner = (band * 2 + side) * BLOCK
            keys = jnp.concatenate(
                [
                    key_f[band, starts[side] : starts[side] + 2 * BLOCK, feats],
                    corner_keys[corner : corner + BLOCK, feats],
                ],
                axis=0,
            )
            query = head_pair(query_ref[first : first + BLOCK, feats])
            return lax.dot_general(keys, query, NT, preferred_element_type=F32)

        def weighed(unit, scores):
            return soft(scores)

        def summed(unit, held):
            side, pair, band = unit
            weights, highest, total = held
            feats = slice(pair * 128, pair * 128 + 128)
            corner = (band * 2 + side) * BLOCK
            values = jnp.concatenate(
                [
                    value_f[band, feats, starts[side] : starts[side] + 2 * BLOCK],
                    corner_values[feats, corner : corner + BLOCK],
                ],
                axis=1,
            )
            mixed = jnp.dot(values, weights, preferred_element_type=F32)
            waiting[unit] = (mixed, jnp.where(beyond[band], NEG, highest), total)
            if band == 0:
                return
            upper = waiting.pop((side, pair, 0))
            lower = waiting.pop(unit)
            for h in range(2):
                here = (slice(h * BLOCK, (h + 1) * BLOCK), slice(None), slice(None))
                tiles = [join(x[part], y[part], h == 1) for x, y, part in zip(upper, lower, here)]
                at = side * (SECTORS - 1) * COLUMN
                lanes = slice(side * COLUMN, (side + 1) * COLUMN)

                def store(rows, value):
                    att_ref[rows, lanes] = value

                merge(tiles, pair * 2 + h, slice(at, at + COLUMN), near_refs, store)

        waiting = {}
        staged(
            [
                (side, pair, band)
                for side in range(2)
                for pair in range(PAIRS)
                for band in range(BANDS)
            ],
            (scored, weighed, summed),
        )
        update = lax.dot_general(att_ref[...], out_w[...], TN, preferred_element_type=F32)
        gain = gain_ref[...]
        for side in range(2):
            at = side * (CELLS - COLUMN)
            hidden = hidden_ref[at : at + COLUMN, :] + update[side * COLUMN : (side + 1) * COLUMN]
            if last:
                edge_ref[side * COLUMN : (side + 1) * COLUMN, :] = hidden
                continue
            new_ref[at : at + COLUMN, :] = hidden
            normed = norm_rows(hidden, gain)
            store_normed(at // COLUMN, normed, refs)
        if last:
            for side in range(2):
                for band in range(BANDS):
                    for r in range(8):
                        at = side * COLUMN + band * BLOCK + r * 8
                        side_ref[side, band * 8 + r] = edge_ref[at : at + 8, :].astype(BF16)
                copies[1 + side].start()
            for copy in copies:
                copy.wait()

    return edge_kernel


def edges(query, parts, first, second, hidden, gain, w_key, w_value, w_out, inner, last):
    new, key_f, value_f, *normed = inner
    scratch = [pltpu.VMEM((D, 2 * COLUMN), BF16)]
    if last:
        scratch = [
            pltpu.VMEM((2 * COLUMN, D), F32),
            pltpu.VMEM((16, 48, D), BF16),
            pltpu.VMEM((2, 16, 8, D), BF16),
            pltpu.SemaphoreType.DMA((3,)),
        ] + scratch
        out_shape = jax.ShapeDtypeStruct((16, 64, D), BF16)
        out_specs = HBM
        aliases = {}
    else:
        out_shape = (pltpu.VMEM((CELLS, D), F32),) + NORMED_SHAPES
        out_specs = (VMEM,) * 6
        aliases = {13: 0, 14: 1, 15: 2, 16: 3}
    return pl.pallas_call(
        make_edge_kernel(last),
        out_shape=out_shape,
        in_specs=[VMEM] * (14 + len(normed)),
        out_specs=out_specs,
        scratch_shapes=scratch,
        input_output_aliases=aliases,
        compiler_params=PARAMS,
        name="edges",
    )(query, *parts, first, second, hidden, gain, w_key, w_value, w_out, key_f, value_f, new, *normed)


def local(
    obs_feat, obs_owner, obs_cell, obs_valid, grid_feat,
    w_embed, gains, w_query, w_key, w_value, w_out,
):
    send = dispatch(
        off_chip(obs_owner.reshape(1, OBS)),
        off_chip(obs_cell.reshape(1, OBS)),
        off_chip(obs_valid.reshape(1, OBS)),
        off_chip(obs_feat),
    )
    got = lax.all_to_all(on_chip(send), ("lat", "lon"), split_axis=0, concat_axis=0, tiled=True)
    lat_count = lax.axis_size("lat")
    lon_count = lax.axis_size("lon")
    hidden, *normed = combine(got, off_chip(w_embed), off_chip(grid_feat), gains)
    lat_first = [(i, i ^ 1) for i in range(lat_count)]
    lat_second = [(0, 0), (lat_count - 1, lat_count - 1)]
    for i in range(1, lat_count - 1, 2):
        lat_second += [(i, i + 1), (i + 1, i)]
    lat_round = [(i, (((i + 1) ^ 1) - 1) % lat_count) for i in range(lat_count)]
    lon_first = [(i, i ^ 1) for i in range(lon_count)]
    lon_second = [(i, (((i + 1) ^ 1) - 1) % lon_count) for i in range(lon_count)]
    for layer in range(LAYERS):
        last = layer == LAYERS - 1
        key_w = on_chip(w_key[layer])
        value_w = on_chip(jnp.transpose(w_value[layer]))
        hidden = on_chip(hidden)
        flat, *trades = [on_chip(item) for item in normed]
        third = lax.ppermute(trades[2], "lon", lon_first)
        fourth = lax.ppermute(trades[3], "lon", lon_second)
        second = lax.ppermute(trades[1], "lat", lat_second)
        first = lax.ppermute(trades[0], "lat", lat_first)
        query, key, value, *parts = project(flat, on_chip(w_query[layer]), key_w, value_w)
        query = on_chip(query)
        corner = corners(third, fourth)
        corner_second = lax.ppermute(on_chip(corner[1]), "lat", lat_round)
        corner_first = lax.ppermute(on_chip(corner[0]), "lat", lat_first)
        parts = [on_chip(part) for part in parts]
        parts = near(
            query, on_chip(key), on_chip(value), third, fourth, key_w, value_w, parts
        )
        parts = [on_chip(part) for part in parts]
        following = min(layer + 1, LAYERS - 1)
        gain = gains[following : following + 1]
        out_w = on_chip(w_out[layer])
        inner = far(query, parts, first, second, hidden, gain, key_w, value_w, out_w, last)
        inner = [on_chip(item) for item in inner]
        result = edges(
            query, parts, corner_first, corner_second, hidden, gain, key_w, value_w, out_w, inner, last
        )
        if not last:
            hidden, *normed = result
    return result


def solution(mesh):
    placed = (
        P(("lat", "lon"), None),
        P(("lat", "lon"), None),
        P(("lat", "lon")),
        P(("lat", "lon")),
        P("lat", "lon", None),
        P(), P(), P(), P(), P(), P(),
    )
    return jax.shard_map(
        local, mesh=mesh, in_specs=placed, out_specs=P("lat", "lon", None), check_vma=False
    )
```

```python
import jax
import jax.numpy as jnp
from jax import lax
from jax.experimental import pallas as pl
from jax.experimental.pallas import tpu as pltpu
from jax.sharding import PartitionSpec as P

HEADS = 8
LAYERS = 2
D = 512
FIN = 256
DEVICES = 128
CAP = 16
ROWS = 40
OBS = 1024
CELLS = 1024
SLOTS = DEVICES * CAP
BLOCK = 64
BANDS = 2
SECTORS = 8
FRAME = SECTORS + 2
PAIRS = HEADS // 2
COLUMN = BANDS * BLOCK
NEG = -1e30
F32 = jnp.float32
BF16 = jnp.bfloat16

VMEM = pl.BlockSpec(memory_space=pltpu.VMEM)
HBM = pl.BlockSpec(memory_space=pl.ANY)
PARAMS = pltpu.CompilerParams(vmem_limit_bytes=40 * 1024 * 1024)
WIDE = FRAME * BLOCK
HALO = SECTORS * BLOCK
NT = (((1,), (1,)), ((), ()))
TN = (((0,), (0,)), ((), ()))


def iota(shape, axis):
    return lax.broadcasted_iota(jnp.int32, shape, axis)


def dispatch_kernel(
    owner_hbm, cell_hbm, valid_hbm, feat_hbm, send_ref, owner_ref, cell_ref, valid_ref, feat_ref, sems
):
    pairs = ((owner_hbm, owner_ref), (cell_hbm, cell_ref), (valid_hbm, valid_ref), (feat_hbm, feat_ref))
    copies = [pltpu.make_async_copy(a, b, sems.at[i]) for i, (a, b) in enumerate(pairs)]
    for copy in copies:
        copy.start()
    for copy in copies[:3]:
        copy.wait()
    owner = owner_ref[...]
    cell = cell_ref[...]
    valid = valid_ref[...]
    wide = 256
    earlier = (iota((wide, wide), 0) < iota((wide, wide), 1)).astype(F32).astype(BF16)
    carry = jnp.zeros((DEVICES, 1), F32)
    ranks = []
    chosen = []
    for at in range(0, OBS, wide):
        hot = (iota((DEVICES, wide), 0) == owner[:, at : at + wide]).astype(F32)
        before = jnp.dot(hot.astype(BF16), earlier, preferred_element_type=F32) + carry
        ranks.append(jnp.sum(hot * before, axis=0, keepdims=True))
        carry = carry + jnp.sum(hot, axis=1, keepdims=True)
        chosen.append(hot.astype(BF16))
    rank = jnp.concatenate(ranks, axis=1).astype(jnp.int32)
    hot_all = jnp.concatenate(chosen, axis=1)
    row = cell // 64
    col = cell % 64
    high = (col // 8) * BANDS + row // 8 + 1
    low = (row % 8) * 8 + col % 8
    usable = valid == 1
    high = jnp.where(usable, high, 0)
    low = jnp.where(usable, low, 0)
    lane = iota((128, OBS), 0)
    part = jnp.where(lane < CAP, high, jnp.where(lane < 2 * CAP, low, 0))
    entry = jnp.where(lane % CAP == rank, part, 0).astype(F32).astype(BF16)
    tags = lax.dot_general(hot_all, entry, NT, preferred_element_type=F32)
    send_ref[:, 32:40, :] = jnp.broadcast_to(tags[:, None, :], (DEVICES, 8, 128)).astype(BF16)
    target = owner * CAP + rank
    copies[3].wait()
    feat = feat_ref[...]
    step = 1024
    for at in range(0, SLOTS, step):
        pick = (iota((step, OBS), 0) + at == target).astype(F32).astype(BF16)
        rows = jnp.dot(pick, feat, preferred_element_type=F32).astype(BF16)
        first = at // CAP
        count = step // CAP
        send_ref[first : first + count, 0:16, :] = rows[:, :128].reshape(count, CAP, 128)
        send_ref[first : first + count, 16:32, :] = rows[:, 128:].reshape(count, CAP, 128)


def dispatch(owner, cell, valid, feat):
    return pl.pallas_call(
        dispatch_kernel,
        out_shape=pltpu.VMEM((DEVICES, ROWS, 128), BF16),
        in_specs=[HBM] * 4,
        out_specs=VMEM,
        scratch_shapes=[pltpu.VMEM((1, OBS), jnp.int32)] * 3
        + [pltpu.VMEM((OBS, FIN), BF16), pltpu.SemaphoreType.DMA((4,))],
        compiler_params=PARAMS,
        name="dispatch",
    )(owner, cell, valid, feat)


def on_chip(array):
    return pltpu.with_memory_space_constraint(array, pltpu.VMEM)


def off_chip(array):
    return pltpu.with_memory_space_constraint(array, pltpu.HBM)


def norm_rows(hidden, gain):
    scale = lax.rsqrt(jnp.mean(hidden * hidden, axis=-1, keepdims=True) + 1e-06)
    return (hidden * scale * gain).astype(BF16)


def pick(choose, x, y):
    return jnp.where(choose, x, y)


def store_normed(sector, rows, refs):
    normed_ref, first_ref, second_ref, third_ref, fourth_ref = refs
    here = slice(sector * BLOCK, (sector + 1) * BLOCK)
    normed_ref[sector * COLUMN : (sector + 1) * COLUMN, :] = rows
    even = lax.axis_index("lat") % 2 == 0
    top = rows[:BLOCK]
    low = rows[BLOCK:]
    first_ref[here, :] = pick(even, low, top)
    second_ref[here, :] = pick(even, top, low)
    if sector == 0:
        third_ref[...] = rows
        fourth_ref[...] = rows
    if sector == SECTORS - 1:
        even = lax.axis_index("lon") % 2 == 0
        third_ref[...] = pick(even, rows, third_ref[...])
        fourth_ref[...] = pick(even, fourth_ref[...], rows)


NORMED_SHAPES = (
    pltpu.VMEM((CELLS, D), BF16),
    pltpu.VMEM((HALO, D), BF16),
    pltpu.VMEM((HALO, D), BF16),
    pltpu.VMEM((COLUMN, D), BF16),
    pltpu.VMEM((COLUMN, D), BF16),
)


def gelu(x):
    inner = x * (0.7978845608028654 + (0.7978845608028654 * 0.044715) * (x * x))
    half = 0.5 * x
    return half + half * jnp.tanh(inner)


def combine_kernel(
    got_ref, embed_hbm, grid_hbm, gain_ref, hidden_ref, *rest
):
    refs = rest[:5]
    emb_ref, tag_ref, hot_ref, embed_ref, grid_ref, sems = rest[5:]
    fetch_embed = pltpu.make_async_copy(embed_hbm, embed_ref, sems.at[0])
    fetch_grid = pltpu.make_async_copy(grid_hbm, grid_ref, sems.at[1])
    fetch_embed.start()
    fetch_grid.start()
    tag_ref[...] = got_ref[:, 32:40, :].astype(F32).reshape(DEVICES * 8, 128)
    tags = tag_ref[pl.ds(0, DEVICES, stride=8), :]
    tags = jnp.transpose(tags)[: 2 * CAP].astype(BF16)
    spread = (iota((DEVICES, SLOTS), 1) // CAP == iota((DEVICES, SLOTS), 0)).astype(F32).astype(BF16)
    wide = jnp.dot(tags, spread, preferred_element_type=F32)
    own = iota((CAP, SLOTS), 1) % CAP == iota((CAP, SLOTS), 0)
    high = jnp.sum(jnp.where(own, wide[:CAP], 0.0), axis=0, keepdims=True)
    low = jnp.sum(jnp.where(own, wide[CAP:], 0.0), axis=0, keepdims=True)
    low_hot = (iota((BLOCK, SLOTS), 0).astype(F32) == low).astype(F32).astype(BF16)
    high_hot = (iota((16, SLOTS), 0).astype(F32) + 1.0 == high).astype(F32).astype(BF16)
    counts = lax.dot_general(low_hot, high_hot, NT, preferred_element_type=F32)
    inverse = 1.0 / jnp.maximum(counts, 1.0)
    high16 = jnp.broadcast_to(high, (16, SLOTS))
    for block in range(BANDS * SECTORS):
        mask = (high16 == block + 1.0).astype(F32).astype(BF16)
        for part in range(BLOCK // 16):
            at = block * BLOCK + part * 16
            hot_ref[at : at + 16, :] = low_hot[part * 16 : part * 16 + 16] * mask
    fetch_embed.wait()
    step = 512
    for at in range(0, SLOTS, step):
        first = at // CAP
        count = step // CAP
        left = got_ref[first : first + count, 0:16, :].reshape(step, 128)
        right = got_ref[first : first + count, 16:32, :].reshape(step, 128)
        raw = jnp.concatenate([left, right], axis=1)
        product = jnp.dot(raw, embed_ref[...], preferred_element_type=F32)
        emb_ref[at : at + step, :] = gelu(product).astype(BF16)
    gain = gain_ref[0:1, :]
    fetch_grid.wait()
    chunk = 1024
    for start in range(0, CELLS, chunk):
        total = jnp.dot(hot_ref[start : start + chunk, :], emb_ref[...], preferred_element_type=F32)
        for sub in range(chunk // COLUMN):
            sector = start // COLUMN + sub
            pieces = []
            for band in range(BANDS):
                block = sector * BANDS + band
                row = sub * COLUMN + band * BLOCK
                mean = total[row : row + BLOCK] * inverse[:, block : block + 1]
                static = jnp.concatenate(
                    [
                        grid_ref[band * 8 + r, sector * 8 : sector * 8 + 8, :].astype(F32)
                        for r in range(8)
                    ],
                    axis=0,
                )
                pieces.append(mean + static)
            hidden = jnp.concatenate(pieces, axis=0)
            hidden_ref[sector * COLUMN : (sector + 1) * COLUMN, :] = hidden
            store_normed(sector, norm_rows(hidden, gain), refs)


def combine(got, w_embed, grid_feat, gains):
    return pl.pallas_call(
        combine_kernel,
        out_shape=(pltpu.VMEM((CELLS, D), F32),) + NORMED_SHAPES,
        in_specs=[VMEM, HBM, HBM, VMEM],
        out_specs=(VMEM,) * 6,
        scratch_shapes=[
            pltpu.VMEM((SLOTS, D), BF16),
            pltpu.VMEM((DEVICES * 8, 128), F32),
            pltpu.VMEM((CELLS, SLOTS), BF16),
            pltpu.VMEM((FIN, D), BF16),
            pltpu.VMEM((16, 64, D), BF16),
            pltpu.SemaphoreType.DMA((2,)),
        ],
        compiler_params=PARAMS,
        name="combine",
    )(got, w_embed, grid_feat, gains)


def head_pair(query):
    lane = iota(query.shape, 1) < BLOCK
    zero = jnp.zeros_like(query)
    return jnp.concatenate([jnp.where(lane, query, zero), jnp.where(lane, zero, query)], axis=0)


def fold(values, op):
    rows, width = values.shape
    part = op(values.reshape(rows // BLOCK, BLOCK, width), axis=0)
    part = op(part.reshape(8, 8, width), axis=0)
    return op(part, axis=0, keepdims=True)


def soft(scores):
    highest = fold(scores, jnp.max)
    expo = jnp.exp(scores - highest)
    return expo.astype(BF16), highest, fold(expo, jnp.sum)


LAGS = (0, 3, 4)


def staged(units, stages):
    held = {}
    for turn in range(len(units) + LAGS[-1]):
        for lag, stage in zip(LAGS, stages):
            at = turn - lag
            if 0 <= at < len(units):
                held[at] = stage(units[at], held.get(at))


def near_columns(columns, query_ref, mixed_ref, highest_ref, total_ref):
    units = [(sector, pair) for sector in columns for pair in range(PAIRS)]

    def scored(unit, _):
        sector, pair = unit
        feats = slice(pair * 128, pair * 128 + 128)
        query = head_pair(query_ref[sector * COLUMN : (sector + 1) * COLUMN, feats])
        return lax.dot_general(columns[sector][0](feats), query, NT, preferred_element_type=F32)

    def weighed(unit, scores):
        return soft(scores)

    def summed(unit, held):
        sector, pair = unit
        weights, highest, total = held
        feats = slice(pair * 128, pair * 128 + 128)
        mixed = jnp.dot(columns[sector][1](feats), weights, preferred_element_type=F32)
        at = slice(sector * COLUMN, (sector + 1) * COLUMN)
        for h in range(2):
            head = pair * 2 + h
            lanes = slice(h * COLUMN, (h + 1) * COLUMN)
            mixed_ref[head * BLOCK : (head + 1) * BLOCK, at] = mixed[h * BLOCK : (h + 1) * BLOCK, lanes]
            highest_ref[head : head + 1, at] = highest[:, lanes]
            total_ref[head : head + 1, at] = total[:, lanes]

    staged(units, (scored, weighed, summed))


def inner_column(sector, key_ref, value_ref):
    at = slice((sector - 1) * COLUMN, (sector + 2) * COLUMN)
    return (lambda feats: key_ref[at, feats], lambda feats: value_ref[feats, at])


NEAR_SHAPES = (
    pltpu.VMEM((D, CELLS), F32),
    pltpu.VMEM((HEADS, CELLS), F32),
    pltpu.VMEM((HEADS, CELLS), F32),
)


def project_kernel(
    normed_ref, query_w, key_w, value_w,
    query_ref, key_ref, value_ref, mixed_ref, highest_ref, total_ref,
):
    flat = normed_ref[...]
    query = jnp.dot(flat, query_w[...], preferred_element_type=F32).astype(BF16)
    query_ref[...] = query * BF16(0.125)
    key_ref[...] = jnp.dot(flat, key_w[...], preferred_element_type=F32).astype(BF16)
    value_ref[...] = lax.dot_general(value_w[...], flat, NT, preferred_element_type=F32).astype(BF16)
    columns = {sector: inner_column(sector, key_ref, value_ref) for sector in range(1, SECTORS - 1)}
    near_columns(columns, query_ref, mixed_ref, highest_ref, total_ref)


def project(normed, w_query, w_key, w_value):
    shape = pltpu.VMEM((CELLS, D), BF16)
    return pl.pallas_call(
        project_kernel,
        out_shape=(shape, shape, pltpu.VMEM((D, CELLS), BF16)) + NEAR_SHAPES,
        in_specs=[VMEM] * 4,
        out_specs=(VMEM,) * 6,
        compiler_params=PARAMS,
        cost_estimate=pl.CostEstimate(flops=6 * CELLS * D * D, transcendentals=0, bytes_accessed=5 << 20),
        name="project",
    )(normed, w_query, w_key, w_value)


def sides_of(third_ref, fourth_ref):
    even = lax.axis_index("lon") % 2 == 0
    third = third_ref[...]
    fourth = fourth_ref[...]
    return pick(even, fourth, third), pick(even, third, fourth)


def rows_of(first_ref, second_ref):
    even = lax.axis_index("lat") % 2 == 0
    first = first_ref[...]
    second = second_ref[...]
    return pick(even, second, first), pick(even, first, second)


def corners_kernel(third_ref, fourth_ref, first_ref, second_ref):
    west, east = sides_of(third_ref, fourth_ref)
    even = lax.axis_index("lat") % 2 == 0
    top = jnp.concatenate([west[:BLOCK], east[:BLOCK]], axis=0)
    low = jnp.concatenate([west[BLOCK:], east[BLOCK:]], axis=0)
    first_ref[...] = pick(even, low, top)
    second_ref[...] = pick(even, top, low)


def corners(third, fourth):
    shape = pltpu.VMEM((COLUMN, D), BF16)
    return pl.pallas_call(
        corners_kernel,
        out_shape=(shape, shape),
        in_specs=[VMEM] * 2,
        out_specs=(VMEM,) * 2,
        compiler_params=PARAMS,
        name="corners",
    )(third, fourth)


def near_kernel(
    query_ref, key_ref, value_ref, third_ref, fourth_ref, key_w, value_w, mixed_in, highest_in, total_in,
    mixed_ref, highest_ref, total_ref,
):
    del mixed_in, highest_in, total_in
    outs = (query_ref, mixed_ref, highest_ref, total_ref)
    sides = jnp.concatenate(sides_of(third_ref, fourth_ref), axis=0)
    side_keys = jnp.dot(sides, key_w[...], preferred_element_type=F32).astype(BF16)
    side_values = lax.dot_general(value_w[...], sides, NT, preferred_element_type=F32).astype(BF16)
    columns = {}
    inner = 2 * COLUMN
    columns[0] = (
        lambda feats: jnp.concatenate([side_keys[:COLUMN, feats], key_ref[:inner, feats]], axis=0),
        lambda feats: jnp.concatenate(
            [side_values[feats, :COLUMN], value_ref[feats, :inner]], axis=1
        ),
    )
    columns[SECTORS - 1] = (
        lambda feats: jnp.concatenate(
            [key_ref[CELLS - inner :, feats], side_keys[COLUMN:, feats]], axis=0
        ),
        lambda feats: jnp.concatenate(
            [value_ref[feats, CELLS - inner :], side_values[feats, COLUMN:]], axis=1
        ),
    )
    near_columns(columns, *outs)


def near(query, key, value, third, fourth, w_key, w_value, parts):
    return pl.pallas_call(
        near_kernel,
        out_shape=NEAR_SHAPES,
        in_specs=[VMEM] * 10,
        out_specs=(VMEM,) * 3,
        input_output_aliases={7: 0, 8: 1, 9: 2},
        compiler_params=PARAMS,
        cost_estimate=pl.CostEstimate(flops=8 << 30, transcendentals=4 << 20, bytes_accessed=8 << 20),
        name="near",
    )(query, key, value, third, fourth, w_key, w_value, *parts)


def merge(tiles, head, cells, near_refs, store):
    mixed_ref, highest_ref, total_ref = near_refs
    mixed, highest, total = tiles
    rows = slice(head * BLOCK, (head + 1) * BLOCK)
    highest_near = highest_ref[head : head + 1, cells]
    top = jnp.maximum(highest, highest_near)
    near_part = jnp.exp(highest_near - top)
    far_part = jnp.exp(highest - top)
    weight = total_ref[head : head + 1, cells] * near_part + total * far_part
    near_part = near_part / weight
    far_part = far_part / weight
    store(rows, (mixed_ref[rows, cells] * near_part + mixed * far_part).astype(BF16))


def join(x, y, turn_x):
    if turn_x:
        x = pltpu.roll(x, BLOCK, 1)
    else:
        y = pltpu.roll(y, BLOCK, 1)
    return jnp.where(iota(x.shape, 1) < BLOCK, x, y)


def beyond_grid():
    lat = lax.axis_index("lat")
    return (lat == 0, lat == lax.axis_size("lat") - 1)


def make_far_kernel(last):
    def far_kernel(
        query_ref, mixed_ref, highest_ref, total_ref, first_ref, second_ref,
        hidden_ref, gain_ref, key_w, value_w, out_w, *rest,
    ):
        new_ref, key_f, value_f = rest[:3]
        refs = rest[3:-1]
        att_ref = rest[-1]
        near_refs = (mixed_ref, highest_ref, total_ref)
        for band, rows in enumerate(rows_of(first_ref, second_ref)):
            key_f[band] = jnp.dot(rows, key_w[...], preferred_element_type=F32).astype(BF16)
            value_f[band] = lax.dot_general(
                value_w[...], rows, NT, preferred_element_type=F32
            ).astype(BF16)
        beyond = beyond_grid()
        span = 4 * BLOCK

        def hide(scores):
            second = iota((BLOCK, 2 * COLUMN), 1) % COLUMN >= BLOCK
            return jnp.concatenate(
                [
                    jnp.where(second, NEG, scores[:BLOCK]),
                    scores[BLOCK : 3 * BLOCK],
                    jnp.where(second, scores[3 * BLOCK :], NEG),
                ],
                axis=0,
            )

        def scored(unit, _):
            step, pair, band = unit
            feats = slice(pair * 128, pair * 128 + 128)
            first = (step * 2 + 1) * COLUMN + band * BLOCK
            query = jnp.concatenate(
                [
                    query_ref[first : first + BLOCK, feats],
                    query_ref[first + COLUMN : first + COLUMN + BLOCK, feats],
                ],
                axis=0,
            )
            keys = key_f[band, step * COLUMN : step * COLUMN + span, feats]
            return hide(lax.dot_general(keys, head_pair(query), NT, preferred_element_type=F32))

        def weighed(unit, scores):
            return soft(scores)

        def summed(unit, held):
            step, pair, band = unit
            weights, highest, total = held
            feats = slice(pair * 128, pair * 128 + 128)
            values = value_f[band, feats, step * COLUMN : step * COLUMN + span]
            mixed = jnp.dot(values, weights, preferred_element_type=F32)
            waiting[unit] = (mixed, jnp.where(beyond[band], NEG, highest), total)
            if band == 0:
                return
            upper = waiting.pop((step, pair, 0))
            lower = waiting.pop(unit)
            for h in range(2):
                lanes = slice(h * COLUMN, (h + 1) * COLUMN)
                here = (slice(h * BLOCK, (h + 1) * BLOCK), slice(None), slice(None))
                for second in range(2):
                    tiles = [
                        join(x[part, lanes], y[part, lanes], second == 1)
                        for x, y, part in zip(upper, lower, here)
                    ]
                    at = (step * 2 + 1 + second) * COLUMN
                    cells = slice(at, at + COLUMN)

                    def store(rows, value):
                        att_ref[rows, cells] = value

                    merge(tiles, pair * 2 + h, cells, near_refs, store)

        waiting = {}
        staged(
            [
                (step, pair, band)
                for step in range(SECTORS // 2 - 1)
                for pair in range(PAIRS)
                for band in range(BANDS)
            ],
            (scored, weighed, summed),
        )
        gain = gain_ref[...]
        for at in range(COLUMN, CELLS - COLUMN, 256):
            update = lax.dot_general(
                att_ref[:, at : at + 256], out_w[...], TN, preferred_element_type=F32
            )
            hidden = hidden_ref[at : at + 256, :] + update
            new_ref[at : at + 256, :] = hidden
            if not last:
                normed = norm_rows(hidden, gain)
                for sub in range(256 // COLUMN):
                    store_normed(
                        at // COLUMN + sub,
                        normed[sub * COLUMN : (sub + 1) * COLUMN],
                        refs + (None, None),
                    )

    return far_kernel


def far(query, parts, first, second, hidden, gain, w_key, w_value, w_out, last):
    out_shape = (
        pltpu.VMEM((CELLS, D), F32),
        pltpu.VMEM((BANDS, HALO, D), BF16),
        pltpu.VMEM((BANDS, D, HALO), BF16),
    )
    if not last:
        out_shape = out_shape + NORMED_SHAPES[:3]
    return pl.pallas_call(
        make_far_kernel(last),
        out_shape=out_shape,
        in_specs=[VMEM] * 11,
        out_specs=(VMEM,) * len(out_shape),
        scratch_shapes=[pltpu.VMEM((D, CELLS), BF16)],
        compiler_params=PARAMS,
        cost_estimate=pl.CostEstimate(flops=8 << 30, transcendentals=4 << 20, bytes_accessed=8 << 20),
        name="far",
    )(query, *parts, first, second, hidden, gain, w_key, w_value, w_out)


def make_edge_kernel(last):
    def edge_kernel(
        query_ref, mixed_ref, highest_ref, total_ref, first_ref, second_ref,
        hidden_ref, gain_ref, key_w, value_w, out_w, key_f, value_f, *rest,
    ):
        near_refs = (mixed_ref, highest_ref, total_ref)
        att_ref = rest[-1]
        if last:
            inner_ref, out_ref, edge_ref, stage_ref, side_ref, sems = rest[:6]
            for band in range(BANDS):
                for r in range(8):
                    pieces = []
                    for sector in range(1, SECTORS - 1):
                        at = (sector * BANDS + band) * BLOCK + r * 8
                        pieces.append(inner_ref[at : at + 8, :])
                    stage_ref[band * 8 + r] = jnp.concatenate(pieces, axis=0).astype(BF16)
            copies = [
                pltpu.make_async_copy(stage_ref, out_ref.at[:, pl.ds(8, 48), :], sems.at[0]),
                pltpu.make_async_copy(side_ref.at[0], out_ref.at[:, pl.ds(0, 8), :], sems.at[1]),
                pltpu.make_async_copy(side_ref.at[1], out_ref.at[:, pl.ds(56, 8), :], sems.at[2]),
            ]
            copies[0].start()
        else:
            new_ref = rest[4]
            refs = rest[5:10]
        rows = jnp.concatenate(rows_of(first_ref, second_ref), axis=0)
        corner_keys = jnp.dot(rows, key_w[...], preferred_element_type=F32).astype(BF16)
        corner_values = lax.dot_general(
            value_w[...], rows, NT, preferred_element_type=F32
        ).astype(BF16)
        beyond = beyond_grid()
        starts = (0, HALO - 2 * BLOCK)

        def scored(unit, _):
            side, pair, band = unit
            feats = slice(pair * 128, pair * 128 + 128)
            first = side * (SECTORS - 1) * COLUMN + band * BLOCK
            corner = (band * 2 + side) * BLOCK
            keys = jnp.concatenate(
                [
                    key_f[band, starts[side] : starts[side] + 2 * BLOCK, feats],
                    corner_keys[corner : corner + BLOCK, feats],
                ],
                axis=0,
            )
            query = head_pair(query_ref[first : first + BLOCK, feats])
            return lax.dot_general(keys, query, NT, preferred_element_type=F32)

        def weighed(unit, scores):
            return soft(scores)

        def summed(unit, held):
            side, pair, band = unit
            weights, highest, total = held
            feats = slice(pair * 128, pair * 128 + 128)
            corner = (band * 2 + side) * BLOCK
            values = jnp.concatenate(
                [
                    value_f[band, feats, starts[side] : starts[side] + 2 * BLOCK],
                    corner_values[feats, corner : corner + BLOCK],
                ],
                axis=1,
            )
            mixed = jnp.dot(values, weights, preferred_element_type=F32)
            waiting[unit] = (mixed, jnp.where(beyond[band], NEG, highest), total)
            if band == 0:
                return
            upper = waiting.pop((side, pair, 0))
            lower = waiting.pop(unit)
            for h in range(2):
                here = (slice(h * BLOCK, (h + 1) * BLOCK), slice(None), slice(None))
                tiles = [join(x[part], y[part], h == 1) for x, y, part in zip(upper, lower, here)]
                at = side * (SECTORS - 1) * COLUMN
                lanes = slice(side * COLUMN, (side + 1) * COLUMN)

                def store(rows, value):
                    att_ref[rows, lanes] = value

                merge(tiles, pair * 2 + h, slice(at, at + COLUMN), near_refs, store)

        waiting = {}
        staged(
            [
                (side, pair, band)
                for side in range(2)
                for pair in range(PAIRS)
                for band in range(BANDS)
            ],
            (scored, weighed, summed),
        )
        update = lax.dot_general(att_ref[...], out_w[...], TN, preferred_element_type=F32)
        gain = gain_ref[...]
        for side in range(2):
            at = side * (CELLS - COLUMN)
            hidden = hidden_ref[at : at + COLUMN, :] + update[side * COLUMN : (side + 1) * COLUMN]
            if last:
                edge_ref[side * COLUMN : (side + 1) * COLUMN, :] = hidden
                continue
            new_ref[at : at + COLUMN, :] = hidden
            normed = norm_rows(hidden, gain)
            store_normed(at // COLUMN, normed, refs)
        if last:
            for side in range(2):
                for band in range(BANDS):
                    for r in range(8):
                        at = side * COLUMN + band * BLOCK + r * 8
                        side_ref[side, band * 8 + r] = edge_ref[at : at + 8, :].astype(BF16)
                copies[1 + side].start()
            for copy in copies:
                copy.wait()

    return edge_kernel


def edges(query, parts, first, second, hidden, gain, w_key, w_value, w_out, inner, last):
    new, key_f, value_f, *normed = inner
    scratch = [pltpu.VMEM((D, 2 * COLUMN), BF16)]
    if last:
        scratch = [
            pltpu.VMEM((2 * COLUMN, D), F32),
            pltpu.VMEM((16, 48, D), BF16),
            pltpu.VMEM((2, 16, 8, D), BF16),
            pltpu.SemaphoreType.DMA((3,)),
        ] + scratch
        out_shape = jax.ShapeDtypeStruct((16, 64, D), BF16)
        out_specs = HBM
        aliases = {}
    else:
        out_shape = (pltpu.VMEM((CELLS, D), F32),) + NORMED_SHAPES
        out_specs = (VMEM,) * 6
        aliases = {13: 0, 14: 1, 15: 2, 16: 3}
    return pl.pallas_call(
        make_edge_kernel(last),
        out_shape=out_shape,
        in_specs=[VMEM] * (14 + len(normed)),
        out_specs=out_specs,
        scratch_shapes=scratch,
        input_output_aliases=aliases,
        compiler_params=PARAMS,
        name="edges",
    )(query, *parts, first, second, hidden, gain, w_key, w_value, w_out, key_f, value_f, new, *normed)


def local(
    obs_feat, obs_owner, obs_cell, obs_valid, grid_feat,
    w_embed, gains, w_query, w_key, w_value, w_out,
):
    send = dispatch(
        off_chip(obs_owner.reshape(1, OBS)),
        off_chip(obs_cell.reshape(1, OBS)),
        off_chip(obs_valid.reshape(1, OBS)),
        off_chip(obs_feat),
    )
    got = lax.all_to_all(on_chip(send), ("lat", "lon"), split_axis=0, concat_axis=0, tiled=True)
    lat_count = lax.axis_size("lat")
    lon_count = lax.axis_size("lon")
    hidden, *normed = combine(got, off_chip(w_embed), off_chip(grid_feat), gains)
    lat_first = [(i, i ^ 1) for i in range(lat_count)]
    lat_second = [(0, 0), (lat_count - 1, lat_count - 1)]
    for i in range(1, lat_count - 1, 2):
        lat_second += [(i, i + 1), (i + 1, i)]
    lat_round = [(i, (((i + 1) ^ 1) - 1) % lat_count) for i in range(lat_count)]
    lon_first = [(i, i ^ 1) for i in range(lon_count)]
    lon_second = [(i, (((i + 1) ^ 1) - 1) % lon_count) for i in range(lon_count)]
    for layer in range(LAYERS):
        last = layer == LAYERS - 1
        key_w = on_chip(w_key[layer])
        value_w = on_chip(jnp.transpose(w_value[layer]))
        hidden = on_chip(hidden)
        flat, *trades = [on_chip(item) for item in normed]
        third = lax.ppermute(trades[2], "lon", lon_first)
        fourth = lax.ppermute(trades[3], "lon", lon_second)
        second = lax.ppermute(trades[1], "lat", lat_second)
        first = lax.ppermute(trades[0], "lat", lat_first)
        query, key, value, *parts = project(flat, on_chip(w_query[layer]), key_w, value_w)
        query = on_chip(query)
        corner = corners(third, fourth)
        corner_second = lax.ppermute(on_chip(corner[1]), "lat", lat_round)
        corner_first = lax.ppermute(on_chip(corner[0]), "lat", lat_first)
        parts = [on_chip(part) for part in parts]
        parts = near(
            query, on_chip(key), on_chip(value), third, fourth, key_w, value_w, parts
        )
        parts = [on_chip(part) for part in parts]
        following = min(layer + 1, LAYERS - 1)
        gain = gains[following : following + 1]
        out_w = on_chip(w_out[layer])
        inner = far(query, parts, first, second, hidden, gain, key_w, value_w, out_w, last)
        inner = [on_chip(item) for item in inner]
        result = edges(
            query, parts, corner_first, corner_second, hidden, gain, key_w, value_w, out_w, inner, last
        )
        if not last:
            hidden, *normed = result
    return result


def solution(mesh):
    placed = (
        P(("lat", "lon"), None),
        P(("lat", "lon"), None),
        P(("lat", "lon")),
        P(("lat", "lon")),
        P("lat", "lon", None),
        P(), P(), P(), P(), P(), P(),
    )
    return jax.shard_map(
        local, mesh=mesh, in_specs=placed, out_specs=P("lat", "lon", None), check_vma=False
    )
```
